512 devices in a mesh: req: 8 (over z), hid: 64 (over y, x, core).
Axes of the slice: x: 4, y: 8, z: 8, core: 2. Of those that a mesh axis runs over, the one named last changes fastest.
Arguments:
- residual_input: bfloat16 [4096, 2048], P('req', 'hid'), may hold values from -6 to 6
- queries: bfloat16 [4096, 2048], P('req'), may hold values from -31 to 31
- key_value_pairs: bfloat16 [4096, 1024], P('req'), may hold values from -4 to 4
- prompt_length_list: int32 [8, 6], P('req'), may hold values from 1 to 320, 512 in all within a row
- prompt_adapter_index: int32 [8, 6], P('req'), may hold values from 0 to 63
- adapter_position: int32 [64], replicated, may hold values from 0 to 63, each once
- output_matrix: bfloat16 [2048, 2048], P('req', 'hid'), may hold values from -0.125 to 0.125
- output_factor_first: bfloat16 [64, 2048, 16], P('hid'), may hold values from -0.125 to 0.125
- output_factor_second: bfloat16 [64, 16, 2048], P(None, None, 'hid'), may hold values from -1.5 to 1.5
- norm_weight: bfloat16 [2048], P('hid'), may hold values from 0.3984375 to 1.59375
- gate_up_matrix: bfloat16 [2048, 2, 8192], P('req', None, 'hid'), may hold values from -0.125 to 0.125
- gate_up_factor_first: bfloat16 [64, 2048, 32], P('hid'), may hold values from -0.125 to 0.125
- gate_up_factor_second: bfloat16 [2, 64, 16, 8192], P(None, None, None, 'hid'), may hold values from -1.5 to 1.5
- down_matrix: bfloat16 [8192, 2048], P('hid', 'req'), may hold values from -0.1875 to 0.1875
- down_factor_first: bfloat16 [8192, 64, 16], P('hid'), may hold values from -0.0625 to 0.0625
- down_factor_second: bfloat16 [64, 16, 2048], P(None, None, 'hid'), may hold values from -1.5 to 1.5
Outputs:
- stream_out: bfloat16 [4096, 2048], P('req', 'hid')
The draws below stay inside these ranges and needn't reach their ends.
Inputs may be any that keep to these rules, and one draw needn't show every extreme that they name: `prompt_length_list`: each row holds the lengths of one group's prompts; a row sums to 512 and its largest entry is exactly 320. `adapter_position`: a permutation of 0 to 63.
All inputs are finite; a program needn't handle non-finite values.
Results may differ from the reference program's by a relative error of at most 0.02.
Values may be sent and summed in bfloat16 or wider, within the bound.
A program may use at most 64 MiB of HBM per device.

```python
import math
import jax
import jax.numpy as jnp
import numpy as np
from jax import lax

MODEL_DIMENSION = 2048
FEEDFORWARD_UNIT = 8192
HEADS = 8
KV_HEADS = 2
HEAD = 256
ADAPTER_RANK = 16
PROMPTS_GRP = 6
TOK_GRP = 512
ADAPTER_TOTAL = 64
TOKENS = 4096
MOST_LEN = 320
N_REQ = 8


def attention_inputs(key):
    key_width = KV_HEADS * HEAD
    key_query = jax.random.fold_in(key, 101)
    key_pairs = jax.random.fold_in(key, 102)
    query_rows = jnp.clip(jax.random.normal(key_query, (TOKENS, HEADS * HEAD), jnp.float32), -4.0, 4.0)
    pair_rows = jnp.clip(jax.random.normal(key_pairs, (TOKENS, 2 * key_width), jnp.float32), -4.0, 4.0)
    return (query_rows.astype(jnp.bfloat16), pair_rows.astype(jnp.bfloat16))


def draw_queries(key, part):
    return attention_inputs(key)[0]


def draw_key_value_pairs(key, part):
    return attention_inputs(key)[1]


def with_ends(drawn, stream_key, low, top_value):
    extent = drawn.shape
    index_at = [jax.random.randint(jax.random.fold_in(stream_key, axis), (), 0, extent[axis]) for axis in range(len(extent))]
    drawn = drawn.at[tuple(index_at)].set(low)
    longest = extent.index(max(extent))
    index_at[longest] = (index_at[longest] + 1) % extent[longest]
    return drawn.at[tuple(index_at)].set(top_value)


def strengthened(values, stream_key, source, target, blocks, factor):
    owner, partner = [(jnp.arange(values.shape[dim]) // (values.shape[dim] // blocks)).reshape([-1 if axis == dim else 1 for axis in range(values.ndim)]) for dim in (source, target)]
    chosen = jax.random.permutation(stream_key, blocks)[partner]
    strong = (owner == chosen) | (owner == (partner + blocks // 2) % blocks)
    return jnp.where(strong, factor * values, values)


def levels(rng, extent, split, least, top_value):
    factor_of = 1.0
    for dim, shards_of in split:
        heights = jax.random.uniform(jax.random.fold_in(jax.random.fold_in(rng, 6), dim), (shards_of,), jnp.float32, least / len(split), top_value / len(split))
        factor_of = factor_of * jnp.repeat(jnp.exp(heights), extent[dim] // shards_of).reshape((-1,) + (1,) * (len(extent) - 1 - dim))
    return factor_of


def length_profile(amount, total, reach, slope):
    loads = [(1 << 20) // math.isqrt(grade ** slope) + 1 for grade in range(2, amount + 1)]
    spare, given = total - reach - (amount - 1), [1] * (amount - 1)
    while spare > 0:
        candidates = [i for i in range(amount - 1) if given[i] < reach]
        whole, budget = sum([loads[i] for i in candidates]), spare
        for i in candidates:
            addition = min(reach - given[i], max(1, budget * loads[i] // whole), spare)
            given[i] = given[i] + addition
            spare = spare - addition
    return np.array([reach] + given)


def uneven_parts(key, count, total, reach, lean):
    if count == 2:
        one = jax.random.randint(key, (), max(1, total - reach), min(reach, total - 1) + 1)
        return jnp.stack([one, total - one])
    sizes = jnp.asarray(length_profile(count, total, reach, lean), jnp.int32)
    couples = (count - 1) // 2
    giver, taker = sizes[1:1 + 2 * couples:2], sizes[2:2 + 2 * couples:2]
    slack = jnp.minimum(giver - 1, reach - taker)
    shifted = jax.random.randint(jax.random.fold_in(key, 1), (couples,), 0, 1 << 20) % (slack + 1)
    sizes = sizes.at[1:1 + 2 * couples:2].set(giver - shifted).at[2:2 + 2 * couples:2].set(taker + shifted)
    return sizes[jax.random.permutation(jax.random.fold_in(key, 2), count)]


def normal_values(rng, extent, spread, most, cuts=(), kind=jnp.bfloat16):
    factor_of = levels(rng, extent, cuts, -0.22, 0.18) if cuts else 1.0
    values = jax.random.normal(rng, extent, jnp.float32) * spread * factor_of
    return jnp.minimum(jnp.maximum(values, -most), most).astype(kind)


def bell_draw_with(key, shape, scale, bound, shards, heavy, kind=jnp.bfloat16):
    values = scale * jax.random.normal(key, shape, jnp.float32)
    if shards:
        values = values * levels(key, shape, shards, -0.22, 0.18)
    return jnp.clip(strengthened(values, jax.random.fold_in(key, 3), *heavy), -bound, bound).astype(kind)


def setup_inputs(seed: int = 0) -> dict:
    splits = jax.random.split(jax.random.key(seed), 17)
    residual_input = normal_values(splits[0], (TOKENS, MODEL_DIMENSION), 1.0, 6.0, ((0, 8), (1, 64)))
    queries = draw_queries(jax.random.fold_in(splits[16], 71), 0)
    key_value_pairs = draw_key_value_pairs(jax.random.fold_in(splits[16], 71), 0)
    prompt_length_list = jax.vmap(lambda own: uneven_parts(own, PROMPTS_GRP, TOK_GRP, MOST_LEN, 2))(jax.random.split(splits[3], N_REQ)).reshape((N_REQ, PROMPTS_GRP)).astype(jnp.int32)
    prompt_adapter_index = with_ends(jax.random.randint(splits[4], (N_REQ, PROMPTS_GRP), 0, ADAPTER_TOTAL), jax.random.fold_in(splits[4], 1), 0, ADAPTER_TOTAL - 1).astype(jnp.int32)
    adapter_position = jax.random.permutation(splits[5], ADAPTER_TOTAL).astype(jnp.int32)
    output_matrix = normal_values(splits[6], (HEADS * HEAD, MODEL_DIMENSION), (HEADS * HEAD) ** -0.5, 0.125, ((0, 8), (1, 64)))
    output_factor_first = normal_values(splits[7], (ADAPTER_TOTAL, HEADS * HEAD, ADAPTER_RANK), (HEADS * HEAD) ** -0.5, 0.125, ((0, 64),))
    output_factor_second = normal_values(splits[8], (ADAPTER_TOTAL, ADAPTER_RANK, MODEL_DIMENSION), ADAPTER_RANK ** -0.5, 1.5, ((2, 64),))
    norm_weight = jnp.clip(1.0 + 0.12 * jax.random.normal(splits[9], (MODEL_DIMENSION,), jnp.float32), 0.3984375, 1.59375).astype(jnp.bfloat16)
    gate_up_matrix = normal_values(splits[10], (MODEL_DIMENSION, 2, FEEDFORWARD_UNIT), MODEL_DIMENSION ** -0.5, 0.125, ((0, 8), (2, 64)))
    gate_up_factor_first = normal_values(splits[11], (ADAPTER_TOTAL, MODEL_DIMENSION, 2 * ADAPTER_RANK), MODEL_DIMENSION ** -0.5, 0.125, ((0, 64),))
    gate_up_factor_second = normal_values(splits[12], (2, ADAPTER_TOTAL, ADAPTER_RANK, FEEDFORWARD_UNIT), ADAPTER_RANK ** -0.5, 1.5, ((3, 64),))
    down_matrix = bell_draw_with(splits[13], (FEEDFORWARD_UNIT, MODEL_DIMENSION), FEEDFORWARD_UNIT ** -0.5, 0.1875, ((0, 64), (1, 8)), (0, 1, 64, 4.0))
    down_factor_first = normal_values(splits[14], (FEEDFORWARD_UNIT, ADAPTER_TOTAL, ADAPTER_RANK), FEEDFORWARD_UNIT ** -0.5, 0.0625, ((0, 64),))
    down_factor_second = normal_values(splits[15], (ADAPTER_TOTAL, ADAPTER_RANK, MODEL_DIMENSION), ADAPTER_RANK ** -0.5, 1.5, ((2, 64),))
    return dict(residual_input=residual_input, queries=queries, key_value_pairs=key_value_pairs, prompt_length_list=prompt_length_list, prompt_adapter_index=prompt_adapter_index, adapter_position=adapter_position, output_matrix=output_matrix, output_factor_first=output_factor_first, output_factor_second=output_factor_second, norm_weight=norm_weight, gate_up_matrix=gate_up_matrix, gate_up_factor_first=gate_up_factor_first, gate_up_factor_second=gate_up_factor_second, down_matrix=down_matrix, down_factor_first=down_factor_first, down_factor_second=down_factor_second)


ADAPTER_SCALE = 0.5
EPS = 1e-06

def pick_rank(full, position_rows, adapter_list, rank):
    shaped = full.reshape(full.shape[0], adapter_list, rank)
    return jnp.take_along_axis(shaped, position_rows[:, None, None], axis=1)[:, 0, :]

def widen_rank(rank_rows, position_rows, adapter_list):
    onehot = (position_rows[:, None] == jnp.arange(adapter_list, dtype=jnp.int32)[None, :]).astype(jnp.bfloat16)
    return (onehot[:, :, None] * rank_rows[:, None, :]).reshape(rank_rows.shape[0], -1)

def reference(residual_input, queries, key_value_pairs, prompt_length_list, prompt_adapter_index, adapter_position, output_matrix, output_factor_first, output_factor_second, norm_weight, gate_up_matrix, gate_up_factor_first, gate_up_factor_second, down_matrix, down_factor_first, down_factor_second):
    group_size = HEADS // KV_HEADS
    key_width = KV_HEADS * HEAD
    adapter_list = adapter_position.shape[0]
    position = jnp.arange(TOK_GRP, dtype=jnp.int32)

    def token_meta(lengths_row, adapter_row):
        bounds = jnp.cumsum(lengths_row)
        segment = lax.optimization_barrier(jnp.sum((position[:, None] >= bounds[None, :]).astype(jnp.int32), axis=1))
        return (segment, adapter_position[adapter_row[segment]])
    segments, slots = jax.vmap(token_meta)(prompt_length_list, prompt_adapter_index)

    def attend(inputs):
        query_rows, pair_rows, segment = inputs
        query_heads = query_rows.astype(jnp.float32).reshape(TOK_GRP, KV_HEADS, group_size, HEAD)
        key_rows = pair_rows[:, :key_width].astype(jnp.float32).reshape(TOK_GRP, KV_HEADS, HEAD)
        value_rows = pair_rows[:, key_width:].astype(jnp.float32).reshape(TOK_GRP, KV_HEADS, HEAD)
        scores = jnp.einsum('tkgd,skd->kgts', query_heads, key_rows) * HEAD ** (-0.5)
        allowed = (segment[:, None] == segment[None, :]) & (position[None, :] <= position[:, None])
        scores = jnp.where(allowed, scores, -1e+30)
        attn_probs = jax.nn.softmax(scores, axis=-1).astype(jnp.bfloat16)
        mixed = jnp.einsum('kgts,skd->tkgd', attn_probs.astype(jnp.float32), value_rows)
        return mixed.reshape(TOK_GRP, HEADS * HEAD).astype(jnp.bfloat16)
    attn = lax.map(attend, (queries.reshape(N_REQ, TOK_GRP, -1), key_value_pairs.reshape(N_REQ, TOK_GRP, -1), segments))
    attn = attn.reshape(TOKENS, HEADS * HEAD)
    position_rows = slots.reshape(TOKENS).astype(jnp.int32)
    out_all = jnp.dot(attn, output_factor_first.transpose(1, 0, 2).reshape(HEADS * HEAD, adapter_list * ADAPTER_RANK), preferred_element_type=jnp.float32)
    out_rank = pick_rank(out_all, position_rows, adapter_list, ADAPTER_RANK).astype(jnp.bfloat16)
    output_primary = jnp.dot(attn, output_matrix, preferred_element_type=jnp.float32)
    output_correction = jnp.dot(widen_rank(out_rank, position_rows, adapter_list), output_factor_second.reshape(adapter_list * ADAPTER_RANK, MODEL_DIMENSION), preferred_element_type=jnp.float32)
    middle_state = (residual_input.astype(jnp.float32) + output_primary + ADAPTER_SCALE * output_correction).astype(jnp.bfloat16)
    wide = middle_state.astype(jnp.float32)
    inverse = lax.rsqrt(lax.optimization_barrier(jnp.mean(wide * wide, axis=1)) + EPS)
    normed = (wide * inverse[:, None] * norm_weight.astype(jnp.float32)[None, :]).astype(jnp.bfloat16)
    gu_all = jnp.dot(normed, gate_up_factor_first.transpose(1, 0, 2).reshape(MODEL_DIMENSION, adapter_list * 2 * ADAPTER_RANK), preferred_element_type=jnp.float32)
    gate_up_rank = pick_rank(gu_all, position_rows, adapter_list, 2 * ADAPTER_RANK).astype(jnp.bfloat16)
    gate_primary = jnp.dot(normed, gate_up_matrix[:, 0, :], preferred_element_type=jnp.float32)
    up_primary = jnp.dot(normed, gate_up_matrix[:, 1, :], preferred_element_type=jnp.float32)
    gate_values = gate_primary + ADAPTER_SCALE * jnp.dot(widen_rank(gate_up_rank[:, :ADAPTER_RANK], position_rows, adapter_list), gate_up_factor_second[0].reshape(adapter_list * ADAPTER_RANK, FEEDFORWARD_UNIT), preferred_element_type=jnp.float32)
    up_projected = up_primary + ADAPTER_SCALE * jnp.dot(widen_rank(gate_up_rank[:, ADAPTER_RANK:], position_rows, adapter_list), gate_up_factor_second[1].reshape(adapter_list * ADAPTER_RANK, FEEDFORWARD_UNIT), preferred_element_type=jnp.float32)
    hidden_state = (jax.nn.gelu(gate_values, approximate=True) * up_projected).astype(jnp.bfloat16)
    down_complete = jnp.dot(hidden_state, down_factor_first.reshape(FEEDFORWARD_UNIT, adapter_list * ADAPTER_RANK), preferred_element_type=jnp.float32)
    down_rank_rows = pick_rank(down_complete, position_rows, adapter_list, ADAPTER_RANK).astype(jnp.bfloat16)
    feedforward_output = jnp.dot(hidden_state, down_matrix, preferred_element_type=jnp.float32)
    down_correction = jnp.dot(widen_rank(down_rank_rows, position_rows, adapter_list), down_factor_second.reshape(adapter_list * ADAPTER_RANK, MODEL_DIMENSION), preferred_element_type=jnp.float32)
    return (middle_state.astype(jnp.float32) + feedforward_output + ADAPTER_SCALE * down_correction).astype(jnp.bfloat16)
```

```python
import functools

import jax
import jax.numpy as jnp
from jax import lax
from jax.experimental import pallas as pl
from jax.experimental.pallas import tpu as pltpu
from jax.sharding import PartitionSpec as P

HEADS = 8
KV_HEADS = 2
HEAD = 256
CHUNK = 32
CORES = 2
GRID_X = 4
ADAPTER_SCALE = 0.5
EPS = 1e-06

MESH = pl.DeviceIdType.MESH
F32 = jnp.float32
BF16 = jnp.bfloat16


def dot(a, b):
    return jnp.dot(a, b, preferred_element_type=F32)


def token_bounds(lengths_ref, count):
    bounds, total = [], 0
    for p in range(count):
        start = total
        total = total + lengths_ref[0, p]
        bounds.append((start, total))
    return bounds


def attention_kernel(prompts, lengths_ref, q_ref, k_ref, v_ref, out_ref):
    tokens = q_ref.shape[0]
    half = tokens // 2
    column = lax.broadcasted_iota(jnp.int32, (1, tokens), 1)
    first = jnp.zeros((1, tokens), jnp.int32)
    for start, _ in token_bounds(lengths_ref, prompts):
        first = jnp.where(column >= start, start, first)
    values = v_ref[...].astype(F32).T.astype(BF16)
    for block in range(2):
        lo, hi = block * half, (block + 1) * half
        scores = lax.dot_general(
            k_ref[:hi, :], q_ref[lo:hi, :], (((1,), (1,)), ((), ())), preferred_element_type=F32
        )
        row = lax.broadcasted_iota(jnp.int32, (hi, half), 0)
        allowed = (row >= first[:, lo:hi]) & (row <= column[:, lo:hi])
        scores = jnp.where(allowed, scores * HEAD ** (-0.5), -1e30)
        top = jnp.max(scores, axis=0, keepdims=True)
        weights = jnp.exp(scores - top)
        total = jnp.sum(weights, axis=0, keepdims=True)
        mixed = dot(values[:, :hi], weights.astype(BF16))
        out_ref[:, lo:hi] = (mixed / total).astype(BF16)


def attention(queries, pairs, lengths):
    tokens = queries.shape[0]
    heads = queries.shape[1] // HEAD
    kv_heads = pairs.shape[1] // (2 * HEAD)
    group = heads // kv_heads
    return pl.pallas_call(
        functools.partial(attention_kernel, lengths.shape[1]),
        grid=(heads,),
        out_shape=jax.ShapeDtypeStruct((heads * HEAD, tokens), BF16),
        in_specs=[
            pl.BlockSpec(memory_space=pltpu.SMEM),
            pl.BlockSpec((tokens, HEAD), lambda h: (0, h)),
            pl.BlockSpec((tokens, HEAD), lambda h: (0, h // group)),
            pl.BlockSpec((tokens, HEAD), lambda h: (0, kv_heads + h // group)),
        ],
        out_specs=pl.BlockSpec((HEAD, tokens), lambda h: (h, 0)),
    )(lengths, queries, pairs, pairs)


class Sems:
    def __init__(self, send, recv, used=0):
        self.send, self.recv, self.used = send, recv, used

    def reserve(self, count):
        part = Sems(self.send, self.recv, self.used)
        self.used += count
        return part

    def again(self):
        return Sems(self.send, self.recv, self.used)

    def take(self):
        n = self.used
        self.used += 1
        return self.send.at[n], self.recv.at[n]


SEMAPHORES = 400


def main_kernel(
    dims,
    lengths_ref,
    adapters_ref,
    places_ref,
    attn_ref,
    residual_ref,
    gain_ref,
    wo_ref,
    ao_ref,
    bo_ref,
    gate_ref,
    up_ref,
    agu_ref,
    bgu_ref,
    down_ref,
    ad_ref,
    bd_ref,
    out_ref,
    wo_all,
    gu_all,
    down_all,
    gathered,
    normed,
    partial,
    pair_in,
    summed,
    ring_out,
    ring_in,
    cross_in,
    last_out,
    last_in,
    rank_pair,
    rank_x,
    rank_xin,
    rank_yin,
    rank_back,
    gu_pair,
    gu_x,
    gu_xin,
    gu_yin,
    gu_back,
    sq_pair,
    sq_x,
    sq_xin,
    sq_yin,
    sq_back,
    down_pair,
    down_x,
    down_xin,
    down_yin,
    down_back,
    send_sems,
    recv_sems,
):
    zs, ys, xs = dims
    tokens = attn_ref.shape[1]
    half = tokens // 2
    width = attn_ref.shape[0]
    prompts = lengths_ref.shape[1]
    z = lax.axis_index("req")
    me = lax.axis_index("hid")
    c = lax.rem(me, CORES)
    x = lax.rem(me // CORES, xs)
    y = me // (CORES * xs)
    sems = Sems(send_sems, recv_sems)

    def at(yy, xx, cc):
        return (z, yy * (xs * CORES) + xx * CORES + cc)

    def mod(value, size):
        return lax.rem(value + size, size)

    partner = at(y, x, 1 - c)

    def to_x(k):
        return at(y, mod(x + k, xs), c)

    def to_y(k):
        return at(mod(y + k, ys), x, c)

    def to_z(k):
        return (mod(z + k, zs), me)

    def copy(src, dst, pair, device):
        made = pltpu.make_async_remote_copy(
            src_ref=src,
            dst_ref=dst,
            send_sem=pair[0],
            recv_sem=pair[1],
            device_id=device,
            device_id_type=MESH,
        )
        return made

    def send(src, dst, pair, device):
        made = copy(src, dst, pair, device)
        made.start()
        return made

    def arrived(dst, pair):
        copy(dst, dst, pair, partner).wait_recv()

    barrier = pltpu.get_barrier_semaphore()
    peers = [partner]
    peers += [to_x(k) for k in range(1, xs)]
    peers += [to_y(k) for k in range(1, ys)]
    peers += [to_z(k) for k in range(1, zs)]
    for peer in peers:
        pl.semaphore_signal(barrier, inc=1, device_id=peer, device_id_type=MESH)

    wo_all[z] = wo_ref[...]
    hidden = gate_ref.shape[1]
    gu_all[z, 0:hidden, :] = gate_ref[...].astype(F32).T.astype(BF16)
    gu_all[z, hidden : 2 * hidden, :] = up_ref[...].astype(F32).T.astype(BF16)
    down_all[z] = down_ref[...].astype(F32).T.astype(BF16)

    column = lax.broadcasted_iota(jnp.int32, (1, tokens), 1)
    slots, members = [], []
    owned = jnp.zeros((1, tokens), F32)
    slot_row = jnp.zeros((1, tokens), jnp.int32)
    for p, (start, stop) in enumerate(token_bounds(lengths_ref, prompts)):
        slot = places_ref[adapters_ref[0, p]]
        inside = (column >= start) & (column < stop)
        slots.append(slot)
        members.append(inside.astype(F32))
        owned = owned + jnp.where(inside, jnp.where(slot == me, 1.0, 0.0), 0.0)
        slot_row = jnp.where(inside, slot, slot_row)
    adapters = bo_ref.shape[2]
    chosen = (lax.broadcasted_iota(jnp.int32, (adapters, tokens), 0) == slot_row).astype(BF16)

    pl.semaphore_wait(barrier, len(peers))

    pending = []
    places = [mod(z + k, zs) for k in range(zs)]
    wo_pairs = [sems.take() for _ in range(zs - 1)]
    for k in range(1, zs):
        pending.append(send(wo_all.at[z], wo_all.at[z], wo_pairs[k - 1], to_z(k)))
    ups, downs = zs // 2, (zs - 1) // 2
    z_pairs = {}
    for way, hops in ((1, ups), (-1, downs)):
        for hop in range(1, hops + 1):
            z_pairs[way, hop] = (sems.take(), sems.take())

    def z_slot(way, hop):
        return (zs - way * hop) % zs

    def z_wait(hop):
        for way, hops in ((1, ups), (-1, downs)):
            if 1 <= hop <= hops:
                k = z_slot(way, hop)
                arrived(gu_all.at[places[k]], z_pairs[way, hop][0])
                arrived(down_all.at[places[k]], z_pairs[way, hop][1])

    def z_step(hop):
        z_wait(hop - 1)
        for way, hops in ((1, ups), (-1, downs)):
            if hop <= hops:
                k = z_slot(way, hop - 1)
                block = gu_all.at[places[k]]
                pending.append(send(block, block, z_pairs[way, hop][0], to_z(way)))
                block = down_all.at[places[k]]
                pending.append(send(block, block, z_pairs[way, hop][1], to_z(way)))

    z_step(1)

    def all_reduce(value, pair_buf, x_buf, xin, yin, back, fillers=()):
        fillers = list(fillers) + [lambda: None] * 4
        kind = pair_buf.dtype
        pair_buf[0] = value[:, :half].astype(kind)
        pair_buf[1] = value[:, half:].astype(kind)
        pair = sems.take()
        first = send(pair_buf.at[1 - c], pair_buf.at[2], pair, partner)
        pending.append(first)
        fillers[0]()
        arrived(pair_buf.at[2], pair)
        total = pair_buf[c].astype(F32) + pair_buf[2].astype(F32)
        x_buf[0] = total.astype(kind)
        pairs = [sems.take() for _ in range(1, xs)]
        for k in range(1, xs):
            pending.append(send(x_buf.at[0], xin.at[k - 1], pairs[k - 1], to_x(k)))
        fillers[1]()
        for k in range(1, xs):
            arrived(xin.at[k - 1], pairs[k - 1])
            total = total + xin[k - 1].astype(F32)
        x_buf[1] = total.astype(kind)
        pairs = [sems.take() for _ in range(1, ys)]
        for k in range(1, ys):
            pending.append(send(x_buf.at[1], yin.at[k - 1], pairs[k - 1], to_y(k)))
        fillers[2]()
        for k in range(1, ys):
            arrived(yin.at[k - 1], pairs[k - 1])
            total = total + yin[k - 1].astype(F32)
        back[c] = total.astype(kind)
        pair = sems.take()
        pending.append(send(back.at[c], back.at[c], pair, partner))
        fillers[3]()
        arrived(back.at[1 - c], pair)
        return jnp.concatenate([back[0], back[1]], axis=1)

    def expand(rank):
        return jnp.concatenate([rank * members[p] for p in range(prompts)], axis=0).astype(BF16)

    def column_correction(b_ref, rank):
        ranks = b_ref.shape[0]
        picked = dot(b_ref[...].reshape(ranks * CHUNK, adapters), chosen)
        total = jnp.zeros((CHUNK, tokens), F32)
        for r in range(ranks):
            total = total + picked[r * CHUNK : (r + 1) * CHUNK] * rank[r : r + 1]
        return total

    attn = attn_ref[...]
    out_part = dot(ao_ref[...], attn) * owned
    held = {}

    def project():
        for k in range(1, zs):
            arrived(wo_all.at[places[zs - k]], wo_pairs[k - 1])
        weights = jnp.concatenate([wo_all[k] for k in range(zs)], axis=1)
        held["main"] = dot(weights, attn)

    out_rank = all_reduce(
        out_part, rank_pair, rank_x, rank_xin, rank_yin, rank_back, [None or (lambda: None), lambda: z_step(2), project]
    ).astype(F32)
    middle = (
        residual_ref[...].astype(F32)
        + held["main"]
        + ADAPTER_SCALE * column_correction(bo_ref, out_rank)
    ).astype(BF16)
    local = middle.astype(F32)
    gain_row = gain_ref[...].astype(F32)
    diagonal = lax.broadcasted_iota(jnp.int32, (CHUNK, CHUNK), 0) == lax.broadcasted_iota(
        jnp.int32, (CHUNK, CHUNK), 1
    )
    gain = jnp.sum(jnp.where(diagonal, gain_row, 0.0), axis=1, keepdims=True)
    gathered[c, y, x] = (local * gain).astype(BF16)

    hops_up, hops_down = ys // 2, (ys - 1) // 2
    branch_copies = max(xs - 1 + xs * (hops_up + hops_down), ys - 1 + ys * (xs - 1))
    row_pairs = [sems.take() for _ in range(ys)]
    gather_sems = sems.reserve(branch_copies)

    def gather_zero():
        sems = gather_sems.again()
        own = gathered.at[0, y, x]
        x_pairs = [None] + [sems.take() for _ in range(1, xs)]
        ring = {
            (way, hop, j): sems.take()
            for way, hops in ((1, hops_up), (-1, hops_down))
            for hop in range(1, hops + 1)
            for j in range(xs)
        }
        sent = []
        for k in range(1, xs):
            sent.append(send(own, own, x_pairs[k], to_x(k)))
        for hop in range(1, max(hops_up, hops_down) + 2):
            for j in range(xs):
                xj = mod(x - j, xs)
                if hop == 1 and j > 0:
                    arrived(gathered.at[0, y, xj], x_pairs[j])
                for way, hops in ((1, hops_up), (-1, hops_down)):
                    block = gathered.at[0, mod(y - way * (hop - 1), ys), xj]
                    if 1 < hop <= hops + 1:
                        arrived(block, ring[way, hop - 1, j])
                    if hop <= hops:
                        sent.append(send(block, block, ring[way, hop, j], to_y(way)))
            ways = (1,) if hop == 1 else (1, -1)
            for way in ways:
                if hop == 1 or hop - 1 <= (hops_up if way == 1 else hops_down):
                    k = (way * (hop - 1)) % ys
                    block = gathered.at[0, mod(y - k, ys)]
                    sent.append(send(block, block, row_pairs[k], partner))
        for made in sent:
            made.wait_send()

    def gather_one():
        sems = gather_sems.again()
        own = gathered.at[1, y, x]
        y_pairs = [None] + [sems.take() for _ in range(1, ys)]
        x_pairs = {(r, k): sems.take() for r in range(ys) for k in range(1, xs)}
        sent = []
        order = sorted(range(ys), key=lambda k: min(k, ys - k))
        for k in order[1:]:
            sent.append(send(own, own, y_pairs[k], to_y(k)))
        for r in order:
            block = gathered.at[1, mod(y - r, ys), x]
            if r > 0:
                arrived(block, y_pairs[r])
            for k in range(1, xs):
                sent.append(send(block, block, x_pairs[r, k], to_x(k)))
        for r in order:
            for k in range(1, xs):
                arrived(gathered.at[1, mod(y - r, ys), mod(x - k, xs)], x_pairs[r, k])
            block = gathered.at[1, mod(y - r, ys)]
            sent.append(send(block, block, row_pairs[r], partner))
        for made in sent:
            made.wait_send()

    def run_gather():
        pl.when(c == 0)(gather_zero)
        pl.when(c == 1)(gather_one)
        for k in range(ys):
            arrived(gathered.at[1 - c, mod(y - k, ys)], row_pairs[k])

    squares = jnp.broadcast_to(jnp.sum(local * local, axis=0, keepdims=True), (8, tokens))
    squares = all_reduce(
        squares, sq_pair, sq_x, sq_xin, sq_yin, sq_back, [lambda: None, lambda: z_step(3), run_gather]
    )[0:1]
    inverse = lax.rsqrt(squares / width + EPS)
    z_step(4)
    per_row = width // ys
    for row in range(ys):
        for col in range(xs):
            for core in range(CORES):
                top = row * per_row + (col * CORES + core) * CHUNK
                block = gathered[core, row, col].astype(F32) * inverse
                normed[top : top + CHUNK, :] = block.astype(BF16)

    gu_part = dot(agu_ref[...], normed[...]) * owned

    def gate_up():
        for hop in range(5, max(ups, downs) + 1):
            z_step(hop)
        z_wait(max(ups, downs))
        weights = jnp.concatenate([gu_all[k] for k in range(zs)], axis=1)
        held["gu"] = dot(weights, normed[...])

    gu_rank = all_reduce(
        gu_part, gu_pair, gu_x, gu_xin, gu_yin, gu_back, [lambda: None, lambda: None, gate_up]
    ).astype(F32)
    ranks = gu_rank.shape[0] // 2

    def hidden_correction(which, rank):
        rows = jnp.concatenate([bgu_ref[which, slot] for slot in slots], axis=0)
        return ADAPTER_SCALE * dot(rows.astype(F32).T.astype(BF16), expand(rank))

    gate = held["gu"][:hidden] + hidden_correction(0, gu_rank[:ranks])
    up = held["gu"][hidden:] + hidden_correction(1, gu_rank[ranks:])
    hidden_state = (jax.nn.gelu(gate, approximate=True) * up).astype(BF16)

    a_rows = jnp.concatenate([ad_ref[slot] for slot in slots], axis=0)
    shares = dot(a_rows, hidden_state)
    down_part = jnp.zeros((ranks, tokens), F32)
    for p in range(prompts):
        down_part = down_part + shares[p * ranks : (p + 1) * ranks] * members[p]

    result = {}

    def scatter_pairs():
        pairs = [sems.take() for _ in range(ys)]
        weights = down_all[...].reshape(width, hidden)
        for row in range(ys):
            block = dot(weights[row * per_row : (row + 1) * per_row], hidden_state).astype(BF16)
            partial[row] = block.reshape(xs, CORES, CHUNK, tokens)
            pending.append(send(partial.at[row, :, 1 - c], pair_in.at[row], pairs[row], partner))
        for row in range(ys):
            arrived(pair_in.at[row], pairs[row])
            summed[row] = (partial[row, :, c].astype(F32) + pair_in[row].astype(F32)).astype(BF16)

    scatter_sems = sems.reserve(branch_copies)

    def scatter_zero():
        sems = scatter_sems.again()
        ring = {
            (way, hop, j): sems.take()
            for way, hops in ((1, hops_up), (-1, hops_down))
            for hop in range(1, hops + 1)
            for j in range(xs)
        }
        x_pairs = [None] + [sems.take() for _ in range(1, xs)]
        slot_of = {}
        for way, hops in ((1, hops_up), (-1, hops_down)):
            for hop in range(1, hops + 1):
                slot_of[way, hop] = len(slot_of)
        sent = []
        for hop in range(1, max(hops_up, hops_down) + 1):
            for j in range(xs):
                for way, hops in ((1, hops_up), (-1, hops_down)):
                    if hop > hops:
                        continue
                    row = mod(y + way * (hops + 1 - hop), ys)
                    n = slot_of[way, hop]
                    if hop == 1:
                        block = summed.at[row, j]
                    else:
                        before = slot_of[way, hop - 1]
                        arrived(ring_in.at[before, j], ring[way, hop - 1, j])
                        total = summed[row, j].astype(F32) + ring_in[before, j].astype(F32)
                        ring_out[n, j] = total.astype(BF16)
                        block = ring_out.at[n, j]
                    sent.append(send(block, ring_in.at[n, j], ring[way, hop, j], to_y(way)))
        for j in range(xs):
            total = summed[y, j].astype(F32)
            for way, hops in ((1, hops_up), (-1, hops_down)):
                if hops > 0:
                    n = slot_of[way, hops]
                    arrived(ring_in.at[n, j], ring[way, hops, j])
                    total = total + ring_in[n, j].astype(F32)
            last_out[j] = total.astype(BF16)
        for k in range(1, xs):
            sent.append(send(last_out.at[mod(x + k, xs)], last_in.at[k], x_pairs[k], to_x(k)))
        total = last_out[x].astype(F32)
        for k in range(1, xs):
            arrived(last_in.at[k], x_pairs[k])
            total = total + last_in[k].astype(F32)
        last_in[0] = total.astype(BF16)
        for made in sent:
            made.wait_send()

    def scatter_one():
        sems = scatter_sems.again()
        x_pairs = {(r, k): sems.take() for r in range(ys) for k in range(1, xs)}
        y_pairs = [None] + [sems.take() for _ in range(1, ys)]
        sent = []
        order = sorted(range(ys), key=lambda k: -min(k, ys - k))
        for r in order:
            row = mod(y + r, ys)
            for k in range(1, xs):
                sent.append(
                    send(summed.at[row, mod(x + k, xs)], cross_in.at[r, k - 1], x_pairs[r, k], to_x(k))
                )
        for r in order:
            total = summed[mod(y + r, ys), x].astype(F32)
            for k in range(1, xs):
                arrived(cross_in.at[r, k - 1], x_pairs[r, k])
                total = total + cross_in[r, k - 1].astype(F32)
            last_out[r] = total.astype(BF16)
            if r > 0:
                sent.append(send(last_out.at[r], last_in.at[r], y_pairs[r], to_y(r)))
        total = last_out[0].astype(F32)
        for r in range(1, ys):
            arrived(last_in.at[r], y_pairs[r])
            total = total + last_in[r].astype(F32)
        last_in[0] = total.astype(BF16)
        for made in sent:
            made.wait_send()

    def run_scatter():
        pl.when(c == 0)(scatter_zero)
        pl.when(c == 1)(scatter_one)

    down_rank = all_reduce(
        down_part,
        down_pair,
        down_x,
        down_xin,
        down_yin,
        down_back,
        [scatter_pairs, lambda: None, run_scatter],
    ).astype(F32)
    down_rank = down_rank.astype(BF16).astype(F32)
    out_ref[...] = (
        middle.astype(F32)
        + last_in[0].astype(F32)
        + ADAPTER_SCALE * column_correction(bd_ref, down_rank)
    ).astype(BF16)
    for made in pending:
        made.wait_send()


def main_call(dims, args):
    zs, ys, xs = dims
    attn = args[3]
    tokens = attn.shape[1]
    width = attn.shape[0]
    half = tokens // 2
    gate = args[9]
    hidden = gate.shape[1]
    span = gate.shape[0]
    down_cols = args[13].shape[1]
    ranks = args[7].shape[0]
    hops = ys // 2 + (ys - 1) // 2
    plane = (ys, xs, CORES, CHUNK, tokens)

    def reduce_buffers(rows, kind):
        return [
            pltpu.VMEM((3, rows, half), kind),
            pltpu.VMEM((2, rows, half), kind),
            pltpu.VMEM((max(xs - 1, 1), rows, half), kind),
            pltpu.VMEM((ys - 1, rows, half), kind),
            pltpu.VMEM((2, rows, half), kind),
        ]

    scratch = [
        pltpu.VMEM((zs, CHUNK, span), BF16),
        pltpu.VMEM((zs, 2 * hidden, span), BF16),
        pltpu.VMEM((zs, down_cols, hidden), BF16),
        pltpu.VMEM((CORES, ys, xs, CHUNK, tokens), BF16),
        pltpu.VMEM((width, tokens), BF16),
        pltpu.VMEM(plane, BF16),
        pltpu.VMEM((ys, xs, CHUNK, tokens), BF16),
        pltpu.VMEM((ys, xs, CHUNK, tokens), BF16),
        pltpu.VMEM((hops, xs, CHUNK, tokens), BF16),
        pltpu.VMEM((hops, xs, CHUNK, tokens), BF16),
        pltpu.VMEM((ys, xs - 1, CHUNK, tokens), BF16),
        pltpu.VMEM((max(xs, ys), CHUNK, tokens), BF16),
        pltpu.VMEM((max(xs, ys), CHUNK, tokens), BF16),
    ]
    scratch += reduce_buffers(ranks, BF16)
    scratch += reduce_buffers(2 * ranks, BF16)
    scratch += reduce_buffers(8, F32)
    scratch += reduce_buffers(ranks, F32)
    scratch += [pltpu.SemaphoreType.DMA((SEMAPHORES,)), pltpu.SemaphoreType.DMA((SEMAPHORES,))]
    smem = pl.BlockSpec(memory_space=pltpu.SMEM)
    vmem = pl.BlockSpec(memory_space=pltpu.VMEM)
    return pl.pallas_call(
        functools.partial(main_kernel, dims),
        out_shape=jax.ShapeDtypeStruct((CHUNK, tokens), BF16),
        in_specs=[smem] * 3 + [vmem] * (len(args) - 3),
        out_specs=vmem,
        scratch_shapes=scratch,
        compiler_params=pltpu.CompilerParams(
            collective_id=0, has_side_effects=True, vmem_limit_bytes=60 * 1024 * 1024
        ),
    )(*args)


def body(
    dims,
    residual_input,
    queries,
    key_value_pairs,
    prompt_length_list,
    prompt_adapter_index,
    adapter_position,
    output_matrix,
    output_factor_first,
    output_factor_second,
    norm_weight,
    gate_up_matrix,
    gate_up_factor_first,
    gate_up_factor_second,
    down_matrix,
    down_factor_first,
    down_factor_second,
):
    attn = attention(queries, key_value_pairs, prompt_length_list)
    args = [
        prompt_length_list,
        prompt_adapter_index,
        adapter_position,
        attn,
        residual_input.T,
        norm_weight.reshape(1, -1),
        output_matrix.T,
        output_factor_first[0].T,
        output_factor_second.transpose(1, 2, 0),
        gate_up_matrix[:, 0, :],
        gate_up_matrix[:, 1, :],
        gate_up_factor_first[0].T,
        gate_up_factor_second,
        down_matrix,
        down_factor_first.transpose(1, 2, 0),
        down_factor_second.transpose(1, 2, 0),
    ]
    return main_call(dims, args).T


def solution(mesh):
    placed = (
        P("req", "hid"),
        P("req", None),
        P("req", None),
        P("req", None),
        P("req", None),
        P(),
        P("req", "hid"),
        P("hid", None, None),
        P(None, None, "hid"),
        P("hid"),
        P("req", None, "hid"),
        P("hid", None, None),
        P(None, None, None, "hid"),
        P("hid", "req"),
        P("hid", None, None),
        P(None, None, "hid"),
    )
    dims = (mesh.shape["req"], mesh.shape["hid"] // (CORES * GRID_X), GRID_X)
    return jax.shard_map(
        functools.partial(body, dims),
        mesh=mesh,
        in_specs=placed,
        out_specs=P("req", "hid"),
        check_vma=False,
    )
```

```python
import functools

import jax
import jax.numpy as jnp
from jax import lax
from jax.experimental import pallas as pl
from jax.experimental.pallas import tpu as pltpu
from jax.sharding import PartitionSpec as P

HEADS = 8
KV_HEADS = 2
HEAD = 256
CHUNK = 32
CORES = 2
GRID_X = 4
ADAPTER_SCALE = 0.5
EPS = 1e-06

MESH = pl.DeviceIdType.MESH
F32 = jnp.float32
BF16 = jnp.bfloat16


def dot(a, b):
    return jnp.dot(a, b, preferred_element_type=F32)


def token_bounds(lengths_ref, count):
    bounds, total = [], 0
    for p in range(count):
        start = total
        total = total + lengths_ref[0, p]
        bounds.append((start, total))
    return bounds


class Sems:
    def __init__(self, send, recv, used=0):
        self.send, self.recv, self.used = send, recv, used

    def reserve(self, count):
        part = Sems(self.send, self.recv, self.used)
        self.used += count
        return part

    def again(self):
        return Sems(self.send, self.recv, self.used)

    def take(self):
        n = self.used
        self.used += 1
        return self.send.at[n], self.recv.at[n]


SEMAPHORES = 400


def main_kernel(
    dims,
    lengths_ref,
    adapters_ref,
    places_ref,
    queries_ref,
    pairs_ref,
    residual_ref,
    gain_ref,
    wo_ref,
    ao_ref,
    bo_ref,
    gate_ref,
    up_ref,
    agu_ref,
    bgu_ref,
    down_ref,
    ad_ref,
    bd_ref,
    out_ref,
    q_all,
    kv_all,
    values_all,
    attn_all,
    wo_all,
    gu_all,
    down_all,
    factors,
    middle_ref,
    gathered,
    normed,
    partial,
    pair_in,
    summed,
    ring_out,
    ring_in,
    cross_in,
    last_out,
    last_in,
    rank_pair,
    rank_x,
    rank_xin,
    rank_yin,
    rank_back,
    gu_pair,
    gu_x,
    gu_xin,
    gu_yin,
    gu_back,
    local_sems,
    send_sems,
    recv_sems,
):
    zs, ys, xs = dims
    heads, tokens, _ = q_all.shape
    kv_heads = values_all.shape[0]
    group = heads // kv_heads
    half = tokens // 2
    width = attn_all.shape[0]
    prompts = lengths_ref.shape[1]
    ranks = ao_ref.shape[0]
    z = lax.axis_index("req")
    me = lax.axis_index("hid")
    c = lax.rem(me, CORES)
    x = lax.rem(me // CORES, xs)
    y = me // (CORES * xs)
    sems = Sems(send_sems, recv_sems)
    pending = []

    def at(yy, xx, cc):
        return (z, yy * (xs * CORES) + xx * CORES + cc)

    def mod(value, size):
        return lax.rem(value + size, size)

    def partner():
        return at(y, x, 1 - c)

    def to_x(k):
        return at(y, mod(x + k, xs), c)

    def to_y(k):
        return at(mod(y + k, ys), x, c)

    def to_z(k):
        return (mod(z + k, zs), me)

    def copy(src, dst, pair, device):
        return pltpu.make_async_remote_copy(
            src_ref=src,
            dst_ref=dst,
            send_sem=pair[0],
            recv_sem=pair[1],
            device_id=device,
            device_id_type=MESH,
        )

    def send(src, dst, pair, device):
        made = copy(src, dst, pair, device)
        made.start()
        return made

    def arrived(dst, pair):
        copy(dst, dst, pair, partner()).wait_recv()

    def launch(make):
        make().start()
        pending.append(make)

    loads = []
    for n in range(2 * kv_heads):
        loads.append(
            pltpu.make_async_copy(
                pairs_ref.at[:, n * HEAD : (n + 1) * HEAD], kv_all.at[n], local_sems.at[n]
            )
        )
    for h in range(heads):
        loads.append(
            pltpu.make_async_copy(
                queries_ref.at[:, h * HEAD : (h + 1) * HEAD],
                q_all.at[h],
                local_sems.at[2 * kv_heads + h],
            )
        )
    for load in loads:
        load.start()

    barrier = pltpu.get_barrier_semaphore()
    peers = [partner()]
    peers += [to_x(k) for k in range(1, xs)]
    peers += [to_y(k) for k in range(1, ys)]
    peers += [to_z(k) for k in range(1, zs)]
    for peer in peers:
        pl.semaphore_signal(barrier, inc=1, device_id=peer, device_id_type=MESH)

    wo_all[z] = wo_ref[...]
    hidden = gate_ref.shape[1]
    down_cols = down_ref.shape[1]
    gu_all[z, 0:hidden, :] = gate_ref[...].astype(F32).T.astype(BF16)
    gu_all[z, hidden : 2 * hidden, :] = up_ref[...].astype(F32).T.astype(BF16)
    down_rows = pl.ds(pl.multiple_of(z * down_cols, down_cols), down_cols)
    down_all[down_rows, :] = down_ref[...].astype(F32).T.astype(BF16)

    column = lax.broadcasted_iota(jnp.int32, (1, tokens), 1)
    adapters = bo_ref.shape[2]
    lane = lax.broadcasted_iota(jnp.int32, (1, 128), 1)
    slots, members = [], []
    owned = jnp.zeros((1, tokens), F32)
    first = jnp.zeros((1, tokens), jnp.int32)
    slot_lane = jnp.full((1, 128), -1, jnp.int32)
    total = 0
    for p in range(prompts):
        start = total
        total = total + lengths_ref[0, p]
        slot = places_ref[adapters_ref[0, p]]
        inside = (column >= start) & (column < total)
        slots.append(slot)
        members.append(inside.astype(F32))
        owned = owned + jnp.where(inside, jnp.where(slot == me, 1.0, 0.0), 0.0)
        first = jnp.where(inside, start, first)
        slot_lane = jnp.where(lane // ranks == p, slot, slot_lane)

    adapter_row = lax.broadcasted_iota(jnp.int32, (adapters, 128), 0)
    out_factor = jnp.zeros((CHUNK, 128), F32)
    down_factor = jnp.zeros((CHUNK, 128), F32)
    for r in range(ranks):
        pick = ((adapter_row == slot_lane) & (lax.rem(lane, ranks) == r)).astype(BF16)
        out_factor = out_factor + dot(bo_ref[r], pick)
        down_factor = down_factor + dot(bd_ref[r], pick)
    diagonal = lax.broadcasted_iota(jnp.int32, (CHUNK, CHUNK), 0) == lax.broadcasted_iota(
        jnp.int32, (CHUNK, CHUNK), 1
    )
    gain = jnp.sum(jnp.where(diagonal, gain_ref[...].astype(F32), 0.0), axis=1, keepdims=True)
    gain_lane = prompts * ranks
    out_factor = jnp.where(lane == gain_lane, gain, out_factor)
    factors[c, y, x] = jnp.concatenate([out_factor, down_factor], axis=1).astype(BF16)

    pl.semaphore_wait(barrier, len(peers))

    places = [mod(z + k, zs) for k in range(zs)]
    wo_pairs = [sems.take() for _ in range(zs - 1)]
    for k in range(1, zs):
        launch(lambda k=k: copy(wo_all.at[z], wo_all.at[z], wo_pairs[k - 1], to_z(k)))
    ups, downs = zs // 2, (zs - 1) // 2
    z_pairs = {}
    for way, hops in ((1, ups), (-1, downs)):
        for hop in range(1, hops + 1):
            z_pairs[way, hop] = (sems.take(), sems.take())

    def z_slot(way, hop):
        return mod(z - way * hop, zs)

    def z_block(way, hop):
        slot = z_slot(way, hop)
        return (
            gu_all.at[slot],
            down_all.at[pl.ds(pl.multiple_of(slot * down_cols, down_cols), down_cols), :],
        )

    def z_wait(hop):
        for way, hops in ((1, ups), (-1, downs)):
            if 1 <= hop <= hops:
                for n, block in enumerate(z_block(way, hop)):
                    arrived(block, z_pairs[way, hop][n])

    def z_step(hop):
        z_wait(hop - 1)
        for way, hops in ((1, ups), (-1, downs)):
            if hop <= hops:
                for n in range(2):

                    def make(way=way, n=n):
                        block = z_block(way, hop - 1)[n]
                        return copy(block, block, z_pairs[way, hop][n], to_z(way))

                    launch(make)

    factor_y = [None] + [sems.take() for _ in range(1, ys)]
    factor_x = {(r, k): sems.take() for r in range(ys) for k in range(1, xs)}
    factor_pair = [sems.take() for _ in range(ys)]
    near_first = sorted(range(ys), key=lambda k: min(k, ys - k))

    def factor_send():
        for k in near_first[1:]:
            launch(lambda k=k: copy(factors.at[c, y, x], factors.at[c, y, x], factor_y[k], to_y(k)))

    def factor_cross():
        for r in near_first:
            if r > 0:
                arrived(factors.at[c, mod(y - r, ys), x], factor_y[r])
            for k in range(1, xs):

                def make(r=r, k=k):
                    block = factors.at[c, mod(y - r, ys), x]
                    return copy(block, block, factor_x[r, k], to_x(k))

                launch(make)

    def factor_share():
        for r in near_first:
            for k in range(1, xs):
                arrived(factors.at[c, mod(y - r, ys), mod(x - k, xs)], factor_x[r, k])

            def make(r=r):
                block = factors.at[c, mod(y - r, ys)]
                return copy(block, block, factor_pair[r], partner())

            launch(make)

    def factor_wait():
        for r in near_first:
            arrived(factors.at[1 - c, mod(y - r, ys)], factor_pair[r])

    factor_send()
    z_step(1)

    for n in range(2 * kv_heads):
        loads[n].wait()
    for n in range(kv_heads):
        values_all[n] = kv_all[kv_heads + n].astype(F32).T.astype(BF16)

    def attend(h, carry):
        kv = h // group
        for block in range(2):
            lo, hi = block * half, (block + 1) * half
            scores = lax.dot_general(
                kv_all[kv, :hi, :],
                q_all[h, lo:hi, :],
                (((1,), (1,)), ((), ())),
                preferred_element_type=F32,
            )
            row = lax.broadcasted_iota(jnp.int32, (hi, half), 0)
            allowed = (row >= first[:, lo:hi]) & (row <= column[:, lo:hi])
            scores = jnp.where(allowed, scores * HEAD ** (-0.5), -1e30)
            top = jnp.max(scores, axis=0, keepdims=True)
            weights = jnp.exp(scores - top)
            total = jnp.sum(weights, axis=0, keepdims=True)
            mixed = dot(values_all[kv, :, :hi], weights.astype(BF16))
            attn_all[pl.ds(pl.multiple_of(h * HEAD, HEAD), HEAD), lo:hi] = (mixed / total).astype(BF16)
        return carry

    def attend_heads(lo, hi):
        for h in range(lo, hi):
            loads[2 * kv_heads + h].wait()
        lax.fori_loop(lo, hi, attend, 0)

    cut_one, cut_two = (heads * 3) // 8, (heads * 6) // 8
    attend_heads(0, cut_one)
    factor_cross()
    attend_heads(cut_one, cut_two)
    z_step(2)
    factor_share()
    attend_heads(cut_two, heads)

    class AllReduce:
        def __init__(self, pair_buf, x_buf, xin, yin, back):
            self.bufs = (pair_buf, x_buf, xin, yin, back)
            self.pairs = [sems.take() for _ in range(2 + (xs - 1) + (ys - 1))]
            self.kind = pair_buf.dtype

        def start(self, value):
            pair_buf = self.bufs[0]
            pair_buf[0] = value[:, :half].astype(self.kind)
            pair_buf[1] = value[:, half:].astype(self.kind)
            launch(lambda: copy(pair_buf.at[1 - c], pair_buf.at[2], self.pairs[0], partner()))

        def cross(self):
            pair_buf, x_buf, xin, yin, back = self.bufs
            arrived(pair_buf.at[2], self.pairs[0])
            x_buf[0] = (pair_buf[c].astype(F32) + pair_buf[2].astype(F32)).astype(self.kind)
            for k in range(1, xs):
                launch(lambda k=k: copy(x_buf.at[0], xin.at[k - 1], self.pairs[k], to_x(k)))

        def along(self):
            pair_buf, x_buf, xin, yin, back = self.bufs
            total = x_buf[0].astype(F32)
            for k in range(1, xs):
                arrived(xin.at[k - 1], self.pairs[k])
                total = total + xin[k - 1].astype(F32)
            x_buf[1] = total.astype(self.kind)
            for k in range(1, ys):
                launch(
                    lambda k=k: copy(x_buf.at[1], yin.at[k - 1], self.pairs[xs - 1 + k], to_y(k))
                )

        def share(self):
            pair_buf, x_buf, xin, yin, back = self.bufs
            total = x_buf[1].astype(F32)
            for k in range(1, ys):
                arrived(yin.at[k - 1], self.pairs[xs - 1 + k])
                total = total + yin[k - 1].astype(F32)
            back[c] = total.astype(self.kind)
            launch(lambda: copy(back.at[c], back.at[c], self.pairs[-1], partner()))

        def result(self):
            back = self.bufs[4]
            arrived(back.at[1 - c], self.pairs[-1])
            return jnp.concatenate([back[0], back[1]], axis=1).astype(F32)

    def expand(rank):
        return jnp.concatenate([rank * members[p] for p in range(prompts)], axis=0).astype(BF16)

    def padded(rows, full):
        return jnp.concatenate([rows, jnp.zeros((full - rows.shape[0], tokens), BF16)], axis=0)

    out_reduce = AllReduce(rank_pair, rank_x, rank_xin, rank_yin, rank_back)
    gu_reduce = AllReduce(gu_pair, gu_x, gu_xin, gu_yin, gu_back)
    attn = attn_all[...]
    out_reduce.start(dot(ao_ref[...], attn) * owned)
    for k in range(1, zs):
        arrived(wo_all.at[places[zs - k]], wo_pairs[k - 1])
    weights = jnp.concatenate([wo_all[k] for k in range(zs)], axis=1)
    base = residual_ref[...].astype(F32) + dot(weights, attn)
    middle_ref[...] = base
    gathered[c, y, x] = base.astype(BF16)
    out_reduce.cross()

    def hops_of(way, j):
        long = (way == 1) == (j < (xs + 1) // 2)
        return ys // 2 if long else (ys - 1) // 2

    most = ys // 2
    ring_keys = [
        (way, hop, j)
        for j in range(xs)
        for way in (1, -1)
        for hop in range(1, hops_of(way, j) + 1)
    ]
    ring_slot = {key: n for n, key in enumerate(ring_keys)}
    branch_copies = max(xs - 1 + len(ring_keys), ys - 1 + ys * (xs - 1))
    row_pairs = [sems.take() for _ in range(ys)]
    gather_sems = sems.reserve(branch_copies)

    def beside_gather():
        z_step(3)
        out_reduce.along()

    def branch(run):
        kept = len(pending)
        run()
        made = pending[kept:]
        del pending[kept:]
        return made

    beside = []

    def gather_zero():
        sems = gather_sems.again()
        own = gathered.at[0, y, x]
        x_pairs = [None] + [sems.take() for _ in range(1, xs)]
        ring = {key: sems.take() for key in ring_keys}
        sent = []
        for k in range(1, xs):
            sent.append(send(own, own, x_pairs[k], to_x(k)))
        shared = []
        for hop in range(1, most + 2):
            for j in range(xs):
                xj = mod(x - j, xs)
                if hop == 1 and j > 0:
                    arrived(gathered.at[0, y, xj], x_pairs[j])
                for way in (1, -1):
                    hops = hops_of(way, j)
                    block = gathered.at[0, mod(y - way * (hop - 1), ys), xj]
                    if 1 < hop <= hops + 1:
                        arrived(block, ring[way, hop - 1, j])
                    if hop <= hops:
                        sent.append(send(block, block, ring[way, hop, j], to_y(way)))
            if hop == 1:
                beside.append(branch(beside_gather))
            for k in ((hop - 1) % ys, (1 - hop) % ys):
                if k not in shared:
                    shared.append(k)
                    if k != ys // 2 or hop == most + 1:
                        block = gathered.at[0, mod(y - k, ys)]
                        sent.append(send(block, block, row_pairs[k], partner()))
        for made in sent:
            made.wait_send()

    def gather_one():
        sems = gather_sems.again()
        own = gathered.at[1, y, x]
        y_pairs = [None] + [sems.take() for _ in range(1, ys)]
        x_pairs = {(r, k): sems.take() for r in range(ys) for k in range(1, xs)}
        sent = []
        for k in near_first[1:]:
            sent.append(send(own, own, y_pairs[k], to_y(k)))
        for r in near_first:
            block = gathered.at[1, mod(y - r, ys), x]
            if r > 0:
                arrived(block, y_pairs[r])
            for k in range(1, xs):
                sent.append(send(block, block, x_pairs[r, k], to_x(k)))
            if r == 0:
                branch(beside_gather)
        for r in near_first:
            for k in range(1, xs):
                arrived(gathered.at[1, mod(y - r, ys), mod(x - k, xs)], x_pairs[r, k])
            block = gathered.at[1, mod(y - r, ys)]
            sent.append(send(block, block, row_pairs[r], partner()))
        for made in sent:
            made.wait_send()

    pl.when(c == 0)(gather_zero)
    pl.when(c == 1)(gather_one)
    pending.extend(beside[0])
    out_reduce.share()
    factor_wait()
    for k in near_first:
        arrived(gathered.at[1 - c, mod(y - k, ys)], row_pairs[k])
    z_step(4)

    out_rank = padded(expand(ADAPTER_SCALE * out_reduce.result()), 128)
    middle_ref[...] += dot(factors[c, y, x, :, :128], out_rank)
    per_row = width // ys
    squares = jnp.zeros((8, tokens), F32)
    for row in range(ys):
        for core in range(CORES):
            block = factors[core, row].reshape(xs * CHUNK, 256)[:, :128]
            full = gathered[core, row].reshape(xs * CHUNK, tokens).astype(F32) + dot(block, out_rank)
            squares = squares + jnp.sum((full * full).reshape(-1, 8, tokens), axis=0)
            scaled = (full * block[:, gain_lane : gain_lane + 1].astype(F32)).astype(BF16)
            for col in range(xs):
                top = row * per_row + (col * CORES + core) * CHUNK
                normed[top : top + CHUNK, :] = scaled[col * CHUNK : (col + 1) * CHUNK]
    squares = jnp.sum(squares, axis=0, keepdims=True)
    inverse = lax.rsqrt(squares / width + EPS)

    gu_reduce.start(dot(agu_ref[...], normed[...]) * (owned * inverse))
    for hop in range(5, most + 1):
        z_step(hop)
    gu_reduce.cross()
    z_wait(max(ups, downs))
    weights = jnp.concatenate([gu_all[k] for k in range(zs)], axis=1)
    gu_reduce.along()
    joint = dot(weights, normed[...]) * inverse
    gu_reduce.share()
    gu_rank = gu_reduce.result()

    def hidden_correction(which, rank):
        rows = jnp.concatenate([bgu_ref[which, slot] for slot in slots], axis=0)
        return ADAPTER_SCALE * dot(rows.astype(F32).T.astype(BF16), expand(rank))

    gate = joint[:hidden] + hidden_correction(0, gu_rank[:ranks])
    up = joint[hidden:] + hidden_correction(1, gu_rank[ranks:])
    hidden_state = (jax.nn.gelu(gate, approximate=True) * up).astype(BF16)

    a_rows = jnp.concatenate([ad_ref[slot] for slot in slots], axis=0)
    shares = ADAPTER_SCALE * dot(a_rows, hidden_state)
    down_rank = jnp.concatenate(
        [shares[p * ranks : (p + 1) * ranks] * members[p] for p in range(prompts)], axis=0
    ).astype(BF16)
    source = jnp.concatenate([hidden_state, padded(down_rank, 128)], axis=0)
    far_first = near_first[::-1]
    share_pairs = [sems.take() for _ in range(ys)]
    scatter_sems = sems.reserve(branch_copies)
    for r in far_first:
        row = mod(y + r, ys)
        weights = down_all[pl.ds(pl.multiple_of(row * per_row, per_row), per_row), :]
        extra = jnp.concatenate(
            [factors[core, row, col, :, 128:] for col in range(xs) for core in range(CORES)], axis=0
        )
        block = dot(jnp.concatenate([weights, extra], axis=1), source).astype(BF16)
        for col in range(xs):
            for core in range(CORES):
                top = (col * CORES + core) * CHUNK
                partial[core, r, col] = block[top : top + CHUNK]
        launch(
            lambda r=r: copy(partial.at[1 - c, r], pair_in.at[r], share_pairs[r], partner())
        )

    def add_pair(r):
        arrived(pair_in.at[r], share_pairs[r])
        summed[r] = (partial[c, r].astype(F32) + pair_in[r].astype(F32)).astype(BF16)

    def scatter_zero():
        sems = scatter_sems.again()
        ring = {key: sems.take() for key in ring_keys}
        x_pairs = [None] + [sems.take() for _ in range(1, xs)]
        sent, added = [], []
        for hop in range(1, most + 1):
            todo = []
            for j in range(xs):
                for way in (1, -1):
                    hops = hops_of(way, j)
                    if hop <= hops:
                        todo.append((j, way, (way * (hops + 1 - hop)) % ys))
            if hop == 1:
                todo.sort(key=lambda item: far_first.index(item[2]))
            for j, way, r in todo:
                if r not in added:
                    add_pair(r)
                    added.append(r)
                n = ring_slot[way, hop, j]
                if hop == 1:
                    block = summed.at[r, j]
                else:
                    before = ring_slot[way, hop - 1, j]
                    arrived(ring_in.at[before], ring[way, hop - 1, j])
                    total = summed[r, j].astype(F32) + ring_in[before].astype(F32)
                    ring_out[n] = total.astype(BF16)
                    block = ring_out.at[n]
                sent.append(send(block, ring_in.at[n], ring[way, hop, j], to_y(way)))
            if hop == 1:
                for r in far_first:
                    if r not in added:
                        add_pair(r)
                        added.append(r)
        for j in range(xs):
            total = summed[0, j].astype(F32)
            for way in (1, -1):
                hops = hops_of(way, j)
                if hops > 0:
                    n = ring_slot[way, hops, j]
                    arrived(ring_in.at[n], ring[way, hops, j])
                    total = total + ring_in[n].astype(F32)
            last_out[j] = total.astype(BF16)
        for k in range(1, xs):
            sent.append(send(last_out.at[mod(x + k, xs)], last_in.at[k], x_pairs[k], to_x(k)))
        total = last_out[x].astype(F32)
        for k in range(1, xs):
            arrived(last_in.at[k], x_pairs[k])
            total = total + last_in[k].astype(F32)
        middle_ref[...] = middle_ref[...].astype(BF16).astype(F32) + total
        for made in sent:
            made.wait_send()

    def scatter_one():
        sems = scatter_sems.again()
        x_pairs = {(r, k): sems.take() for r in range(ys) for k in range(1, xs)}
        y_pairs = [None] + [sems.take() for _ in range(1, ys)]
        sent = []
        for r in far_first:
            add_pair(r)
            for k in range(1, xs):
                sent.append(
                    send(summed.at[r, mod(x + k, xs)], cross_in.at[r, k - 1], x_pairs[r, k], to_x(k))
                )
        for r in far_first:
            total = summed[r, x].astype(F32)
            for k in range(1, xs):
                arrived(cross_in.at[r, k - 1], x_pairs[r, k])
                total = total + cross_in[r, k - 1].astype(F32)
            last_out[r] = total.astype(BF16)
            if r > 0:
                sent.append(send(last_out.at[r], last_in.at[r], y_pairs[r], to_y(r)))
        total = last_out[0].astype(F32)
        for r in range(1, ys):
            arrived(last_in.at[r], y_pairs[r])
            total = total + last_in[r].astype(F32)
        middle_ref[...] = middle_ref[...].astype(BF16).astype(F32) + total
        for made in sent:
            made.wait_send()

    pl.when(c == 0)(scatter_zero)
    pl.when(c == 1)(scatter_one)
    out_ref[...] = middle_ref[...].astype(BF16)
    for make in pending:
        make().wait_send()


def main_call(dims, args):
    zs, ys, xs = dims
    tokens, width = args[3].shape
    heads = width // HEAD
    kv_heads = args[4].shape[1] // (2 * HEAD)
    half = tokens // 2
    gate = args[10]
    hidden = gate.shape[1]
    span = gate.shape[0]
    ranks = args[8].shape[0]
    rings = xs * (ys - 1)

    def reduce_buffers(rows, kind):
        return [
            pltpu.VMEM((3, rows, half), kind),
            pltpu.VMEM((2, rows, half), kind),
            pltpu.VMEM((xs - 1, rows, half), kind),
            pltpu.VMEM((ys - 1, rows, half), kind),
            pltpu.VMEM((2, rows, half), kind),
        ]

    scratch = [
        pltpu.VMEM((heads, tokens, HEAD), BF16),
        pltpu.VMEM((2 * kv_heads, tokens, HEAD), BF16),
        pltpu.VMEM((kv_heads, HEAD, tokens), BF16),
        pltpu.VMEM((width, tokens), BF16),
        pltpu.VMEM((zs, CHUNK, span), BF16),
        pltpu.VMEM((zs, 2 * hidden, span), BF16),
        pltpu.VMEM((width, hidden), BF16),
        pltpu.VMEM((CORES, ys, xs, CHUNK, 256), BF16),
        pltpu.VMEM((CHUNK, tokens), F32),
        pltpu.VMEM((CORES, ys, xs, CHUNK, tokens), BF16),
        pltpu.VMEM((width, tokens), BF16),
        pltpu.VMEM((CORES, ys, xs, CHUNK, tokens), BF16),
        pltpu.VMEM((ys, xs, CHUNK, tokens), BF16),
        pltpu.VMEM((ys, xs, CHUNK, tokens), BF16),
        pltpu.VMEM((rings, CHUNK, tokens), BF16),
        pltpu.VMEM((rings, CHUNK, tokens), BF16),
        pltpu.VMEM((ys, xs - 1, CHUNK, tokens), BF16),
        pltpu.VMEM((max(xs, ys), CHUNK, tokens), BF16),
        pltpu.VMEM((max(xs, ys), CHUNK, tokens), BF16),
    ]
    scratch += reduce_buffers(ranks, BF16)
    scratch += reduce_buffers(2 * ranks, BF16)
    scratch += [
        pltpu.SemaphoreType.DMA((heads + 2 * kv_heads,)),
        pltpu.SemaphoreType.DMA((SEMAPHORES,)),
        pltpu.SemaphoreType.DMA((SEMAPHORES,)),
    ]
    smem = pl.BlockSpec(memory_space=pltpu.SMEM)
    vmem = pl.BlockSpec(memory_space=pltpu.VMEM)
    hbm = pl.BlockSpec(memory_space=pl.ANY)
    return pl.pallas_call(
        functools.partial(main_kernel, dims),
        out_shape=jax.ShapeDtypeStruct((CHUNK, tokens), BF16),
        in_specs=[smem] * 3 + [hbm] * 2 + [vmem] * (len(args) - 5),
        out_specs=vmem,
        scratch_shapes=scratch,
        compiler_params=pltpu.CompilerParams(
            collective_id=0, has_side_effects=True, vmem_limit_bytes=60 * 1024 * 1024
        ),
    )(*args)


def body(
    dims,
    residual_input,
    queries,
    key_value_pairs,
    prompt_length_list,
    prompt_adapter_index,
    adapter_position,
    output_matrix,
    output_factor_first,
    output_factor_second,
    norm_weight,
    gate_up_matrix,
    gate_up_factor_first,
    gate_up_factor_second,
    down_matrix,
    down_factor_first,
    down_factor_second,
):
    args = [
        prompt_length_list,
        prompt_adapter_index,
        adapter_position,
        queries,
        key_value_pairs,
        residual_input.T,
        norm_weight.reshape(1, -1),
        output_matrix.T,
        output_factor_first[0].T,
        output_factor_second.transpose(1, 2, 0),
        gate_up_matrix[:, 0, :],
        gate_up_matrix[:, 1, :],
        gate_up_factor_first[0].T,
        gate_up_factor_second,
        down_matrix,
        down_factor_first.transpose(1, 2, 0),
        down_factor_second.transpose(1, 2, 0),
    ]
    return main_call(dims, args).T


def solution(mesh):
    placed = (
        P("req", "hid"),
        P("req", None),
        P("req", None),
        P("req", None),
        P("req", None),
        P(),
        P("req", "hid"),
        P("hid", None, None),
        P(None, None, "hid"),
        P("hid"),
        P("req", None, "hid"),
        P("hid", None, None),
        P(None, None, None, "hid"),
        P("hid", "req"),
        P("hid", None, None),
        P(None, None, "hid"),
    )
    dims = (mesh.shape["req"], mesh.shape["hid"] // (CORES * GRID_X), GRID_X)
    return jax.shard_map(
        functools.partial(body, dims),
        mesh=mesh,
        in_specs=placed,
        out_specs=P("req", "hid"),
        check_vma=False,
    )
```

```python
import functools

import jax
import jax.numpy as jnp
from jax import lax
from jax.experimental import pallas as pl
from jax.experimental.pallas import tpu as pltpu
from jax.sharding import PartitionSpec as P

HEADS = 8
KV_HEADS = 2
HEAD = 256
CHUNK = 32
CORES = 2
GRID_X = 4
ADAPTER_SCALE = 0.5
EPS = 1e-06

MESH = pl.DeviceIdType.MESH
F32 = jnp.float32
BF16 = jnp.bfloat16


def dot(a, b):
    return jnp.dot(a, b, preferred_element_type=F32)


def token_bounds(lengths_ref, count):
    bounds, total = [], 0
    for p in range(count):
        start = total
        total = total + lengths_ref[0, p]
        bounds.append((start, total))
    return bounds


class Sems:
    def __init__(self, send, recv, used=0):
        self.send, self.recv, self.used = send, recv, used

    def reserve(self, count):
        part = Sems(self.send, self.recv, self.used)
        self.used += count
        return part

    def again(self):
        return Sems(self.send, self.recv, self.used)

    def take(self):
        n = self.used
        self.used += 1
        return self.send.at[n], self.recv.at[n]


SEMAPHORES = 400


def main_kernel(
    dims,
    lengths_ref,
    adapters_ref,
    places_ref,
    queries_ref,
    pairs_ref,
    residual_ref,
    gain_ref,
    wo_ref,
    ao_ref,
    bo_ref,
    gate_up_ref,
    agu_hbm,
    bgu_hbm,
    down_ref,
    ad_hbm,
    bd_ref,
    out_ref,
    agu_ref,
    bgu_ref,
    ad_ref,
    bias_all,
    q_all,
    kv_all,
    values_all,
    attn_all,
    wo_all,
    gu_all,
    down_all,
    factors,
    middle_ref,
    gathered,
    normed,
    partial,
    pair_in,
    summed,
    ring_out,
    ring_in,
    cross_in,
    last_out,
    last_in,
    rank_pair,
    rank_x,
    rank_xin,
    rank_yin,
    rank_back,
    gu_pair,
    gu_x,
    gu_xin,
    gu_yin,
    gu_back,
    local_sems,
    send_sems,
    recv_sems,
):
    zs, ys, xs = dims
    heads, tokens, _ = q_all.shape
    kv_heads = values_all.shape[0]
    group = heads // kv_heads
    half = tokens // 2
    width = attn_all.shape[0]
    prompts = lengths_ref.shape[1]
    ranks = ao_ref.shape[0]
    z = lax.axis_index("req")
    me = lax.axis_index("hid")
    c = lax.rem(me, CORES)
    x = lax.rem(me // CORES, xs)
    y = me // (CORES * xs)
    sems = Sems(send_sems, recv_sems)
    pending = []

    def at(yy, xx, cc):
        return (z, yy * (xs * CORES) + xx * CORES + cc)

    def mod(value, size):
        return lax.rem(value + size, size)

    def partner():
        return at(y, x, 1 - c)

    def to_x(k):
        return at(y, mod(x + k, xs), c)

    def to_y(k):
        return at(mod(y + k, ys), x, c)

    def to_z(k):
        return (mod(z + k, zs), me)

    def copy(src, dst, pair, device):
        return pltpu.make_async_remote_copy(
            src_ref=src,
            dst_ref=dst,
            send_sem=pair[0],
            recv_sem=pair[1],
            device_id=device,
            device_id_type=MESH,
        )

    def send(src, dst, pair, device):
        made = copy(src, dst, pair, device)
        made.start()
        return made

    def arrived(dst, pair):
        copy(dst, dst, pair, partner()).wait_recv()

    def launch(make):
        make().start()
        pending.append(make)

    loads = []
    for n in range(2 * kv_heads):
        loads.append(
            pltpu.make_async_copy(
                pairs_ref.at[:, n * HEAD : (n + 1) * HEAD], kv_all.at[n], local_sems.at[n]
            )
        )
    for h in range(heads):
        loads.append(
            pltpu.make_async_copy(
                queries_ref.at[:, h * HEAD : (h + 1) * HEAD],
                q_all.at[h],
                local_sems.at[2 * kv_heads + h],
            )
        )
    for n, (src, dst) in enumerate(((agu_hbm, agu_ref), (bgu_hbm, bgu_ref), (ad_hbm, ad_ref))):
        loads.append(pltpu.make_async_copy(src, dst, local_sems.at[2 * kv_heads + heads + n]))
    for load in loads:
        load.start()

    barrier = pltpu.get_barrier_semaphore()
    peers = [partner()]
    peers += [to_x(k) for k in range(1, xs)]
    peers += [to_y(k) for k in range(1, ys)]
    peers += [to_z(k) for k in range(1, zs)]
    for peer in peers:
        pl.semaphore_signal(barrier, inc=1, device_id=peer, device_id_type=MESH)

    wo_all[z] = wo_ref[...]
    hidden = gate_up_ref.shape[2]
    down_cols = down_ref.shape[1]
    both = gate_up_ref[...].astype(F32)
    for n in range(2):
        gu_all[z, n * hidden : (n + 1) * hidden, :] = both[:, n, :].T.astype(BF16)
    down_rows = pl.ds(pl.multiple_of(z * down_cols, down_cols), down_cols)
    down_all[down_rows, :] = down_ref[...].astype(F32).T.astype(BF16)

    column = lax.broadcasted_iota(jnp.int32, (1, tokens), 1)
    adapters = bo_ref.shape[2]
    lane = lax.broadcasted_iota(jnp.int32, (1, 128), 1)
    slots, members = [], []
    owned = jnp.zeros((1, tokens), F32)
    first = jnp.zeros((1, tokens), jnp.int32)
    slot_lane = jnp.full((1, 128), -1, jnp.int32)
    total = 0
    for p in range(prompts):
        start = total
        total = total + lengths_ref[0, p]
        slot = places_ref[adapters_ref[0, p]]
        inside = (column >= start) & (column < total)
        slots.append(slot)
        members.append(inside.astype(F32))
        owned = owned + jnp.where(inside, jnp.where(slot == me, 1.0, 0.0), 0.0)
        first = jnp.where(inside, start, first)
        slot_lane = jnp.where(lane // ranks == p, slot, slot_lane)

    pl.semaphore_wait(barrier, len(peers))

    places = [mod(z + k, zs) for k in range(zs)]
    wo_pairs = [sems.take() for _ in range(zs - 1)]
    for k in range(1, zs):
        launch(lambda k=k: copy(wo_all.at[z], wo_all.at[z], wo_pairs[k - 1], to_z(k)))
    ups, downs = zs // 2, (zs - 1) // 2
    z_pairs = {}
    for way, hops in ((1, ups), (-1, downs)):
        for hop in range(1, hops + 1):
            z_pairs[way, hop] = (sems.take(), sems.take())

    def z_slot(way, hop):
        return mod(z - way * hop, zs)

    def z_block(way, hop):
        slot = z_slot(way, hop)
        return (
            gu_all.at[slot],
            down_all.at[pl.ds(pl.multiple_of(slot * down_cols, down_cols), down_cols), :],
        )

    def z_wait(hop):
        for way, hops in ((1, ups), (-1, downs)):
            if 1 <= hop <= hops:
                for n, block in enumerate(z_block(way, hop)):
                    arrived(block, z_pairs[way, hop][n])

    def z_step(hop):
        z_wait(hop - 1)
        for way, hops in ((1, ups), (-1, downs)):
            if hop <= hops:
                for n in range(2):

                    def make(way=way, n=n):
                        block = z_block(way, hop - 1)[n]
                        return copy(block, block, z_pairs[way, hop][n], to_z(way))

                    launch(make)

    factor_y = [None] + [sems.take() for _ in range(1, ys)]
    factor_x = {(r, k): sems.take() for r in range(ys) for k in range(1, xs)}
    factor_pair = [sems.take() for _ in range(ys)]
    near_first = sorted(range(ys), key=lambda k: min(k, ys - k))

    def factor_send():
        for k in near_first[1:]:
            launch(lambda k=k: copy(factors.at[c, y, x], factors.at[c, y, x], factor_y[k], to_y(k)))

    def factor_cross():
        for r in near_first:
            if r > 0:
                arrived(factors.at[c, mod(y - r, ys), x], factor_y[r])
            for k in range(1, xs):

                def make(r=r, k=k):
                    block = factors.at[c, mod(y - r, ys), x]
                    return copy(block, block, factor_x[r, k], to_x(k))

                launch(make)

    def factor_share():
        for r in near_first:
            for k in range(1, xs):
                arrived(factors.at[c, mod(y - r, ys), mod(x - k, xs)], factor_x[r, k])

            def make(r=r):
                block = factors.at[c, mod(y - r, ys)]
                return copy(block, block, factor_pair[r], partner())

            launch(make)

    def factor_wait():
        for r in near_first:
            arrived(factors.at[1 - c, mod(y - r, ys)], factor_pair[r])

    z_step(1)
    adapter_row = lax.broadcasted_iota(jnp.int32, (adapters, 128), 0)
    out_factor = jnp.zeros((CHUNK, 128), F32)
    down_factor = jnp.zeros((CHUNK, 128), F32)
    for r in range(ranks):
        pick = ((adapter_row == slot_lane) & (lax.rem(lane, ranks) == r)).astype(BF16)
        out_factor = out_factor + dot(bo_ref[r], pick)
        down_factor = down_factor + dot(bd_ref[r], pick)
    diagonal = lax.broadcasted_iota(jnp.int32, (CHUNK, CHUNK), 0) == lax.broadcasted_iota(
        jnp.int32, (CHUNK, CHUNK), 1
    )
    gain = jnp.sum(jnp.where(diagonal, gain_ref[...].astype(F32), 0.0), axis=1, keepdims=True)
    gain_lane = prompts * ranks
    out_factor = jnp.where(lane == gain_lane, gain, out_factor)
    factors[c, y, x] = jnp.concatenate([out_factor, down_factor], axis=1).astype(BF16)
    factor_send()

    for n in range(2 * kv_heads):
        loads[n].wait()
    for n in range(kv_heads):
        values_all[n] = kv_all[kv_heads + n].astype(F32).T.astype(BF16)

    row = lax.broadcasted_iota(jnp.int32, (tokens, tokens), 0)
    bias_all[...] = jnp.where((row >= first) & (row <= column), 0.0, -1e30)

    def attend_one(h):
        kv = h // group
        for block in range(2):
            lo, hi = block * half, (block + 1) * half
            scores = lax.dot_general(
                kv_all[kv, :hi, :],
                q_all[h, lo:hi, :],
                (((1,), (1,)), ((), ())),
                preferred_element_type=F32,
            )
            scores = scores * HEAD ** (-0.5) + bias_all[:hi, lo:hi]
            top = jnp.max(scores, axis=0, keepdims=True)
            weights = jnp.exp(scores - top)
            total = jnp.sum(weights, axis=0, keepdims=True)
            mixed = dot(values_all[kv, :, :hi], weights.astype(BF16))
            attn_all[pl.ds(pl.multiple_of(h * HEAD, HEAD), HEAD), lo:hi] = (mixed / total).astype(BF16)

    def attend(n, carry):
        attend_one(2 * n)
        attend_one(2 * n + 1)
        return carry

    def attend_heads(lo, hi):
        for h in range(lo, hi):
            loads[2 * kv_heads + h].wait()
        lax.fori_loop(lo // 2, hi // 2, attend, 0)

    cut = 2 * ((heads * 3) // 8)
    attend_heads(0, cut)
    z_step(2)
    factor_cross()
    attend_heads(cut, heads)

    class AllReduce:
        def __init__(self, pair_buf, x_buf, xin, yin, back):
            self.bufs = (pair_buf, x_buf, xin, yin, back)
            self.pairs = [sems.take() for _ in range(2 + (xs - 1) + (ys - 1))]
            self.kind = pair_buf.dtype

        def start(self, value):
            pair_buf = self.bufs[0]
            pair_buf[0] = value[:, :half].astype(self.kind)
            pair_buf[1] = value[:, half:].astype(self.kind)
            launch(lambda: copy(pair_buf.at[1 - c], pair_buf.at[2], self.pairs[0], partner()))

        def cross(self):
            pair_buf, x_buf, xin, yin, back = self.bufs
            arrived(pair_buf.at[2], self.pairs[0])
            x_buf[0] = (pair_buf[c].astype(F32) + pair_buf[2].astype(F32)).astype(self.kind)
            for k in range(1, xs):
                launch(lambda k=k: copy(x_buf.at[0], xin.at[k - 1], self.pairs[k], to_x(k)))

        def along(self):
            pair_buf, x_buf, xin, yin, back = self.bufs
            total = x_buf[0].astype(F32)
            for k in range(1, xs):
                arrived(xin.at[k - 1], self.pairs[k])
                total = total + xin[k - 1].astype(F32)
            x_buf[1] = total.astype(self.kind)
            for k in range(1, ys):
                launch(
                    lambda k=k: copy(x_buf.at[1], yin.at[k - 1], self.pairs[xs - 1 + k], to_y(k))
                )

        def share(self):
            pair_buf, x_buf, xin, yin, back = self.bufs
            total = x_buf[1].astype(F32)
            for k in range(1, ys):
                arrived(yin.at[k - 1], self.pairs[xs - 1 + k])
                total = total + yin[k - 1].astype(F32)
            back[c] = total.astype(self.kind)
            launch(lambda: copy(back.at[c], back.at[c], self.pairs[-1], partner()))

        def result(self):
            back = self.bufs[4]
            arrived(back.at[1 - c], self.pairs[-1])
            return jnp.concatenate([back[0], back[1]], axis=1).astype(F32)

    def expand(rank):
        return jnp.concatenate([rank * members[p] for p in range(prompts)], axis=0).astype(BF16)

    def padded(rows, full):
        return jnp.concatenate([rows, jnp.zeros((full - rows.shape[0], tokens), BF16)], axis=0)

    out_reduce = AllReduce(rank_pair, rank_x, rank_xin, rank_yin, rank_back)
    gu_reduce = AllReduce(gu_pair, gu_x, gu_xin, gu_yin, gu_back)
    attn = attn_all[...]
    out_reduce.start(dot(ao_ref[...], attn) * owned)
    for k in range(1, zs):
        arrived(wo_all.at[places[zs - k]], wo_pairs[k - 1])
    weights = jnp.concatenate([wo_all[k] for k in range(zs)], axis=1)
    base = residual_ref[...].astype(F32) + dot(weights, attn)
    middle_ref[...] = base
    gathered[c, y, x] = base.astype(BF16)
    out_reduce.cross()

    def hops_of(way, j):
        long = (way == 1) == (j < (xs + 1) // 2)
        return ys // 2 if long else (ys - 1) // 2

    most = ys // 2
    ring_keys = [
        (way, hop, j)
        for j in range(xs)
        for way in (1, -1)
        for hop in range(1, hops_of(way, j) + 1)
    ]
    ring_slot = {key: n for n, key in enumerate(ring_keys)}
    branch_copies = max(xs - 1 + len(ring_keys), ys - 1 + ys * (xs - 1))
    row_pairs = [sems.take() for _ in range(ys)]
    gather_sems = sems.reserve(branch_copies)

    def beside_gather():
        out_reduce.along()
        factor_share()
        z_step(3)

    def late_gather():
        z_step(4)

    def branch(run):
        kept = len(pending)
        run()
        made = pending[kept:]
        del pending[kept:]
        return made

    beside = []

    def gather_zero():
        sems = gather_sems.again()
        own = gathered.at[0, y, x]
        x_pairs = [None] + [sems.take() for _ in range(1, xs)]
        ring = {key: sems.take() for key in ring_keys}
        sent = []
        for k in range(1, xs):
            sent.append(send(own, own, x_pairs[k], to_x(k)))
        shared = []
        for hop in range(1, most + 2):
            for j in range(xs):
                xj = mod(x - j, xs)
                if hop == 1 and j > 0:
                    arrived(gathered.at[0, y, xj], x_pairs[j])
                for way in (1, -1):
                    hops = hops_of(way, j)
                    block = gathered.at[0, mod(y - way * (hop - 1), ys), xj]
                    if 1 < hop <= hops + 1:
                        arrived(block, ring[way, hop - 1, j])
                    if hop <= hops:
                        sent.append(send(block, block, ring[way, hop, j], to_y(way)))
            if hop == 1:
                beside.append(branch(beside_gather))
            if hop == most:
                beside.append(branch(late_gather))
            for k in ((hop - 1) % ys, (1 - hop) % ys):
                if k not in shared:
                    shared.append(k)
                    if k != ys // 2 or hop == most + 1:
                        block = gathered.at[0, mod(y - k, ys)]
                        sent.append(send(block, block, row_pairs[k], partner()))
        for made in sent:
            made.wait_send()

    def gather_one():
        sems = gather_sems.again()
        own = gathered.at[1, y, x]
        y_pairs = [None] + [sems.take() for _ in range(1, ys)]
        x_pairs = {(r, k): sems.take() for r in range(ys) for k in range(1, xs)}
        sent = []
        for k in near_first[1:]:
            sent.append(send(own, own, y_pairs[k], to_y(k)))
        for r in near_first:
            block = gathered.at[1, mod(y - r, ys), x]
            if r > 0:
                arrived(block, y_pairs[r])
            for k in range(1, xs):
                sent.append(send(block, block, x_pairs[r, k], to_x(k)))
            if r == 0:
                branch(beside_gather)
        for n, r in enumerate(near_first):
            if n == ys // 2:
                branch(late_gather)
            for k in range(1, xs):
                arrived(gathered.at[1, mod(y - r, ys), mod(x - k, xs)], x_pairs[r, k])
            block = gathered.at[1, mod(y - r, ys)]
            sent.append(send(block, block, row_pairs[r], partner()))
        for made in sent:
            made.wait_send()

    pl.when(c == 0)(gather_zero)
    pl.when(c == 1)(gather_one)
    pending.extend(beside[0] + beside[1])
    out_reduce.share()
    factor_wait()
    for k in near_first:
        arrived(gathered.at[1 - c, mod(y - k, ys)], row_pairs[k])

    out_rank = padded(expand(ADAPTER_SCALE * out_reduce.result()), 128)
    middle_ref[...] += dot(factors[c, y, x, :, :128], out_rank)
    per_row = width // ys
    squares = jnp.zeros((8, tokens), F32)
    for row in range(ys):
        for core in range(CORES):
            block = factors[core, row].reshape(xs * CHUNK, 256)[:, :128]
            full = gathered[core, row].reshape(xs * CHUNK, tokens).astype(F32) + dot(block, out_rank)
            squares = squares + jnp.sum((full * full).reshape(-1, 8, tokens), axis=0)
            scaled = (full * block[:, gain_lane : gain_lane + 1].astype(F32)).astype(BF16)
            for col in range(xs):
                top = row * per_row + (col * CORES + core) * CHUNK
                normed[top : top + CHUNK, :] = scaled[col * CHUNK : (col + 1) * CHUNK]
    squares = jnp.sum(squares, axis=0, keepdims=True)
    inverse = lax.rsqrt(squares / width + EPS)

    for load in loads[2 * kv_heads + heads :]:
        load.wait()
    gu_reduce.start(dot(agu_ref[...], normed[...]) * (owned * inverse))
    for hop in range(5, most + 1):
        z_step(hop)
    gu_reduce.cross()
    z_wait(max(ups, downs))
    weights = jnp.concatenate([gu_all[k] for k in range(zs)], axis=1)
    gu_reduce.along()
    joint = dot(weights, normed[...]) * inverse
    gu_reduce.share()
    gu_rank = gu_reduce.result()

    def hidden_correction(which, rank):
        rows = jnp.concatenate([bgu_ref[which, slot] for slot in slots], axis=0)
        return ADAPTER_SCALE * dot(rows.astype(F32).T.astype(BF16), expand(rank))

    gate = joint[:hidden] + hidden_correction(0, gu_rank[:ranks])
    up = joint[hidden:] + hidden_correction(1, gu_rank[ranks:])
    hidden_state = (jax.nn.gelu(gate, approximate=True) * up).astype(BF16)

    a_rows = jnp.concatenate([ad_ref[slot] for slot in slots], axis=0)
    shares = ADAPTER_SCALE * dot(a_rows, hidden_state)
    down_rank = jnp.concatenate(
        [shares[p * ranks : (p + 1) * ranks] * members[p] for p in range(prompts)], axis=0
    ).astype(BF16)
    source = jnp.concatenate([hidden_state, padded(down_rank, 128)], axis=0)
    far_first = near_first[::-1]
    share_pairs = [sems.take() for _ in range(ys)]
    scatter_sems = sems.reserve(branch_copies)
    for r in far_first:
        row = mod(y + r, ys)
        weights = down_all[pl.ds(pl.multiple_of(row * per_row, per_row), per_row), :]
        extra = jnp.concatenate(
            [factors[core, row, col, :, 128:] for col in range(xs) for core in range(CORES)], axis=0
        )
        block = dot(jnp.concatenate([weights, extra], axis=1), source).astype(BF16)
        for col in range(xs):
            for core in range(CORES):
                top = (col * CORES + core) * CHUNK
                partial[core, r, col] = block[top : top + CHUNK]
        launch(
            lambda r=r: copy(partial.at[1 - c, r], pair_in.at[r], share_pairs[r], partner())
        )

    def add_pair(r):
        arrived(pair_in.at[r], share_pairs[r])
        summed[r] = (partial[c, r].astype(F32) + pair_in[r].astype(F32)).astype(BF16)

    def scatter_zero():
        sems = scatter_sems.again()
        ring = {key: sems.take() for key in ring_keys}
        x_pairs = [None] + [sems.take() for _ in range(1, xs)]
        sent, added = [], []
        for hop in range(1, most + 1):
            todo = []
            for j in range(xs):
                for way in (1, -1):
                    hops = hops_of(way, j)
                    if hop <= hops:
                        todo.append((j, way, (way * (hops + 1 - hop)) % ys))
            if hop == 1:
                todo.sort(key=lambda item: far_first.index(item[2]))
            for j, way, r in todo:
                if r not in added:
                    add_pair(r)
                    added.append(r)
                n = ring_slot[way, hop, j]
                if hop == 1:
                    block = summed.at[r, j]
                else:
                    before = ring_slot[way, hop - 1, j]
                    arrived(ring_in.at[before], ring[way, hop - 1, j])
                    total = summed[r, j].astype(F32) + ring_in[before].astype(F32)
                    ring_out[n] = total.astype(BF16)
                    block = ring_out.at[n]
                sent.append(send(block, ring_in.at[n], ring[way, hop, j], to_y(way)))
            if hop == 1:
                for r in far_first:
                    if r not in added:
                        add_pair(r)
                        added.append(r)
        for j in range(xs):
            total = summed[0, j].astype(F32)
            for way in (1, -1):
                hops = hops_of(way, j)
                if hops > 0:
                    n = ring_slot[way, hops, j]
                    arrived(ring_in.at[n], ring[way, hops, j])
                    total = total + ring_in[n].astype(F32)
            last_out[j] = total.astype(BF16)
        for k in range(1, xs):
            sent.append(send(last_out.at[mod(x + k, xs)], last_in.at[k], x_pairs[k], to_x(k)))
        total = last_out[x].astype(F32)
        for k in range(1, xs):
            arrived(last_in.at[k], x_pairs[k])
            total = total + last_in[k].astype(F32)
        middle_ref[...] = middle_ref[...].astype(BF16).astype(F32) + total
        for made in sent:
            made.wait_send()

    def scatter_one():
        sems = scatter_sems.again()
        x_pairs = {(r, k): sems.take() for r in range(ys) for k in range(1, xs)}
        y_pairs = [None] + [sems.take() for _ in range(1, ys)]
        sent = []
        for r in far_first:
            add_pair(r)
            for k in range(1, xs):
                sent.append(
                    send(summed.at[r, mod(x + k, xs)], cross_in.at[r, k - 1], x_pairs[r, k], to_x(k))
                )
        for r in far_first:
            total = summed[r, x].astype(F32)
            for k in range(1, xs):
                arrived(cross_in.at[r, k - 1], x_pairs[r, k])
                total = total + cross_in[r, k - 1].astype(F32)
            last_out[r] = total.astype(BF16)
            if r > 0:
                sent.append(send(last_out.at[r], last_in.at[r], y_pairs[r], to_y(r)))
        total = last_out[0].astype(F32)
        for r in range(1, ys):
            arrived(last_in.at[r], y_pairs[r])
            total = total + last_in[r].astype(F32)
        middle_ref[...] = middle_ref[...].astype(BF16).astype(F32) + total
        for made in sent:
            made.wait_send()

    pl.when(c == 0)(scatter_zero)
    pl.when(c == 1)(scatter_one)
    out_ref[...] = middle_ref[...].astype(BF16)
    for make in pending:
        make().wait_send()


def main_call(dims, args):
    zs, ys, xs = dims
    tokens, width = args[3].shape
    heads = width // HEAD
    kv_heads = args[4].shape[1] // (2 * HEAD)
    half = tokens // 2
    span, _, hidden = args[10].shape
    ranks = args[8].shape[0]
    rings = xs * (ys - 1)

    def reduce_buffers(rows, kind):
        return [
            pltpu.VMEM((3, rows, half), kind),
            pltpu.VMEM((2, rows, half), kind),
            pltpu.VMEM((xs - 1, rows, half), kind),
            pltpu.VMEM((ys - 1, rows, half), kind),
            pltpu.VMEM((2, rows, half), kind),
        ]

    scratch = [
        pltpu.VMEM(args[11].shape, BF16),
        pltpu.VMEM(args[12].shape, BF16),
        pltpu.VMEM(args[14].shape, BF16),
        pltpu.VMEM((tokens, tokens), F32),
        pltpu.VMEM((heads, tokens, HEAD), BF16),
        pltpu.VMEM((2 * kv_heads, tokens, HEAD), BF16),
        pltpu.VMEM((kv_heads, HEAD, tokens), BF16),
        pltpu.VMEM((width, tokens), BF16),
        pltpu.VMEM((zs, CHUNK, span), BF16),
        pltpu.VMEM((zs, 2 * hidden, span), BF16),
        pltpu.VMEM((width, hidden), BF16),
        pltpu.VMEM((CORES, ys, xs, CHUNK, 256), BF16),
        pltpu.VMEM((CHUNK, tokens), F32),
        pltpu.VMEM((CORES, ys, xs, CHUNK, tokens), BF16),
        pltpu.VMEM((width, tokens), BF16),
        pltpu.VMEM((CORES, ys, xs, CHUNK, tokens), BF16),
        pltpu.VMEM((ys, xs, CHUNK, tokens), BF16),
        pltpu.VMEM((ys, xs, CHUNK, tokens), BF16),
        pltpu.VMEM((rings, CHUNK, tokens), BF16),
        pltpu.VMEM((rings, CHUNK, tokens), BF16),
        pltpu.VMEM((ys, xs - 1, CHUNK, tokens), BF16),
        pltpu.VMEM((max(xs, ys), CHUNK, tokens), BF16),
        pltpu.VMEM((max(xs, ys), CHUNK, tokens), BF16),
    ]
    scratch += reduce_buffers(ranks, BF16)
    scratch += reduce_buffers(2 * ranks, BF16)
    scratch += [
        pltpu.SemaphoreType.DMA((heads + 2 * kv_heads + 3,)),
        pltpu.SemaphoreType.DMA((SEMAPHORES,)),
        pltpu.SemaphoreType.DMA((SEMAPHORES,)),
    ]
    smem = pl.BlockSpec(memory_space=pltpu.SMEM)
    vmem = pl.BlockSpec(memory_space=pltpu.VMEM)
    hbm = pl.BlockSpec(memory_space=pl.ANY)
    return pl.pallas_call(
        functools.partial(main_kernel, dims),
        out_shape=jax.ShapeDtypeStruct((CHUNK, tokens), BF16),
        in_specs=[smem] * 3 + [hbm] * 2 + [vmem] * 6 + [hbm] * 2 + [vmem, hbm, vmem],
        out_specs=vmem,
        scratch_shapes=scratch,
        compiler_params=pltpu.CompilerParams(
            collective_id=0, has_side_effects=True, vmem_limit_bytes=60 * 1024 * 1024
        ),
    )(*args)


def body(
    dims,
    residual_input,
    queries,
    key_value_pairs,
    prompt_length_list,
    prompt_adapter_index,
    adapter_position,
    output_matrix,
    output_factor_first,
    output_factor_second,
    norm_weight,
    gate_up_matrix,
    gate_up_factor_first,
    gate_up_factor_second,
    down_matrix,
    down_factor_first,
    down_factor_second,
):
    args = [
        prompt_length_list,
        prompt_adapter_index,
        adapter_position,
        queries,
        key_value_pairs,
        residual_input.T,
        norm_weight.reshape(1, -1),
        output_matrix.T,
        output_factor_first[0].T,
        output_factor_second.transpose(1, 2, 0),
        gate_up_matrix,
        gate_up_factor_first[0].T,
        gate_up_factor_second,
        down_matrix,
        down_factor_first.transpose(1, 2, 0),
        down_factor_second.transpose(1, 2, 0),
    ]
    return main_call(dims, args).T


def solution(mesh):
    placed = (
        P("req", "hid"),
        P("req", None),
        P("req", None),
        P("req", None),
        P("req", None),
        P(),
        P("req", "hid"),
        P("hid", None, None),
        P(None, None, "hid"),
        P("hid"),
        P("req", None, "hid"),
        P("hid", None, None),
        P(None, None, None, "hid"),
        P("hid", "req"),
        P("hid", None, None),
        P(None, None, "hid"),
    )
    dims = (mesh.shape["req"], mesh.shape["hid"] // (CORES * GRID_X), GRID_X)
    return jax.shard_map(
        functools.partial(body, dims),
        mesh=mesh,
        in_specs=placed,
        out_specs=P("req", "hid"),
        check_vma=False,
    )
```

```python
import functools

import jax
import jax.numpy as jnp
from jax import lax
from jax.experimental import pallas as pl
from jax.experimental.pallas import tpu as pltpu
from jax.sharding import PartitionSpec as P

HEADS = 8
KV_HEADS = 2
HEAD = 256
CHUNK = 32
CORES = 2
GRID_X = 4
ADAPTER_SCALE = 0.5
EPS = 1e-06

MESH = pl.DeviceIdType.MESH
F32 = jnp.float32
BF16 = jnp.bfloat16


def dot(a, b):
    return jnp.dot(a, b, preferred_element_type=F32)


def token_bounds(lengths_ref, count):
    bounds, total = [], 0
    for p in range(count):
        start = total
        total = total + lengths_ref[0, p]
        bounds.append((start, total))
    return bounds


class Sems:
    def __init__(self, send, recv, used=0):
        self.send, self.recv, self.used = send, recv, used

    def take(self):
        n = self.used
        self.used += 1
        return self.send.at[n], self.recv.at[n]


SEMAPHORES = 400


def main_kernel(
    dims,
    lengths_ref,
    adapters_ref,
    places_ref,
    queries_ref,
    pairs_ref,
    residual_ref,
    gain_ref,
    wo_ref,
    ao_ref,
    bo_ref,
    gate_up_ref,
    agu_hbm,
    bgu_hbm,
    down_ref,
    ad_hbm,
    bd_ref,
    out_ref,
    agu_ref,
    bgu_ref,
    ad_ref,
    bias_all,
    q_all,
    kv_all,
    values_all,
    attn_all,
    wo_all,
    gu_all,
    down_all,
    factors,
    middle_ref,
    gathered,
    normed,
    partial,
    pair_in,
    summed,
    near_in,
    away_in,
    on_out,
    on_in,
    last_out,
    last_in,
    rank_pair,
    rank_x,
    rank_xin,
    rank_yin,
    rank_back,
    gu_pair,
    gu_x,
    gu_xin,
    gu_yin,
    gu_back,
    local_sems,
    send_sems,
    recv_sems,
):
    zs, ys, xs = dims
    heads, tokens, _ = q_all.shape
    kv_heads = values_all.shape[0]
    group = heads // kv_heads
    half = tokens // 2
    width = attn_all.shape[0]
    prompts = lengths_ref.shape[1]
    ranks = ao_ref.shape[0]
    z = lax.axis_index("req")
    me = lax.axis_index("hid")
    c = lax.rem(me, CORES)
    x = lax.rem(me // CORES, xs)
    y = me // (CORES * xs)
    sems = Sems(send_sems, recv_sems)
    pending = []

    def at(yy, xx, cc):
        return (z, yy * (xs * CORES) + xx * CORES + cc)

    def mod(value, size):
        return lax.rem(value + size, size)

    def partner():
        return at(y, x, 1 - c)

    def to_x(k):
        return at(y, mod(x + k, xs), c)

    def to_y(k):
        return at(mod(y + k, ys), x, c)

    def to_z(k):
        return (mod(z + k, zs), me)

    def copy(src, dst, pair, device):
        return pltpu.make_async_remote_copy(
            src_ref=src,
            dst_ref=dst,
            send_sem=pair[0],
            recv_sem=pair[1],
            device_id=device,
            device_id_type=MESH,
        )

    def arrived(dst, pair):
        copy(dst, dst, pair, partner()).wait_recv()

    def launch(make):
        make().start()
        pending.append(make)

    loads = []
    for n in range(2 * kv_heads):
        loads.append(
            pltpu.make_async_copy(
                pairs_ref.at[:, n * HEAD : (n + 1) * HEAD], kv_all.at[n], local_sems.at[n]
            )
        )
    for h in range(heads):
        loads.append(
            pltpu.make_async_copy(
                queries_ref.at[:, h * HEAD : (h + 1) * HEAD],
                q_all.at[h],
                local_sems.at[2 * kv_heads + h],
            )
        )
    for n, (src, dst) in enumerate(((agu_hbm, agu_ref), (bgu_hbm, bgu_ref), (ad_hbm, ad_ref))):
        loads.append(pltpu.make_async_copy(src, dst, local_sems.at[2 * kv_heads + heads + n]))
    for load in loads:
        load.start()

    barrier = pltpu.get_barrier_semaphore()
    peers = [partner()]
    peers += [to_x(k) for k in range(1, xs)]
    peers += [to_y(k) for k in range(1, ys)]
    peers += [to_z(k) for k in range(1, zs)]
    for peer in peers:
        pl.semaphore_signal(barrier, inc=1, device_id=peer, device_id_type=MESH)

    wo_all[z] = wo_ref[...]
    hidden = gate_up_ref.shape[2]
    down_cols = down_ref.shape[1]

    column = lax.broadcasted_iota(jnp.int32, (1, tokens), 1)
    adapters = bo_ref.shape[2]
    lane = lax.broadcasted_iota(jnp.int32, (1, 128), 1)
    slots, members = [], []
    owned = jnp.zeros((1, tokens), F32)
    first = jnp.zeros((1, tokens), jnp.int32)
    slot_lane = jnp.full((1, 128), -1, jnp.int32)
    total = 0
    for p in range(prompts):
        start = total
        total = total + lengths_ref[0, p]
        slot = places_ref[adapters_ref[0, p]]
        inside = (column >= start) & (column < total)
        slots.append(slot)
        members.append(inside.astype(F32))
        owned = owned + jnp.where(inside, jnp.where(slot == me, 1.0, 0.0), 0.0)
        first = jnp.where(inside, start, first)
        slot_lane = jnp.where(lane // ranks == p, slot, slot_lane)

    adapter_row = lax.broadcasted_iota(jnp.int32, (adapters, 128), 0)
    out_factor = jnp.zeros((CHUNK, 128), F32)
    down_factor = jnp.zeros((CHUNK, 128), F32)
    for r in range(ranks):
        pick = ((adapter_row == slot_lane) & (lax.rem(lane, ranks) == r)).astype(BF16)
        out_factor = out_factor + dot(bo_ref[r], pick)
        down_factor = down_factor + dot(bd_ref[r], pick)
    diagonal = lax.broadcasted_iota(jnp.int32, (CHUNK, CHUNK), 0) == lax.broadcasted_iota(
        jnp.int32, (CHUNK, CHUNK), 1
    )
    gain = jnp.sum(jnp.where(diagonal, gain_ref[...].astype(F32), 0.0), axis=1, keepdims=True)
    gain_lane = prompts * ranks
    out_factor = jnp.where(lane == gain_lane, gain, out_factor)
    factors[c, y, x] = jnp.concatenate([out_factor, down_factor], axis=1).astype(BF16)

    pl.semaphore_wait(barrier, len(peers))

    places = [mod(z + k, zs) for k in range(zs)]
    wo_pairs = [sems.take() for _ in range(zs - 1)]
    ups, downs = zs // 2, (zs - 1) // 2
    z_pairs = {}
    for way, hops in ((1, ups), (-1, downs)):
        for hop in range(1, hops + 1):
            z_pairs[way, hop] = (sems.take(), sems.take())

    def z_slot(way, hop):
        return mod(z - way * hop, zs)

    def z_block(way, hop):
        slot = z_slot(way, hop)
        return (
            gu_all.at[slot],
            down_all.at[pl.ds(pl.multiple_of(slot * down_cols, down_cols), down_cols), :],
        )

    def z_wait(hop):
        for way, hops in ((1, ups), (-1, downs)):
            if 1 <= hop <= hops:
                for n, block in enumerate(z_block(way, hop)):
                    arrived(block, z_pairs[way, hop][n])

    def z_step(hop):
        z_wait(hop - 1)
        for way, hops in ((1, ups), (-1, downs)):
            if hop <= hops:
                for n in range(2):

                    def make(way=way, n=n):
                        block = z_block(way, hop - 1)[n]
                        return copy(block, block, z_pairs[way, hop][n], to_z(way))

                    launch(make)

    near_first = sorted(range(ys), key=lambda k: min(k, ys - k))
    far_first = near_first[::-1]
    ways = (1, -1) if xs > 2 else (1,)

    def side(r):
        return 1 if r % 2 == 0 else -1

    class Gather:
        def __init__(self, buf):
            self.buf = buf
            self.y_pairs = [None] + [sems.take() for _ in range(1, ys)]
            self.x_pairs = {(r, way): sems.take() for r in range(ys) for way in ways}
            self.far_pairs = [sems.take() for _ in range(ys)]
            self.core_pairs = [sems.take() for _ in range(ys)]

        def block(self, r, k):
            return self.buf.at[c, mod(y - r, ys), mod(x + k, xs)]

        def send(self):
            for k in near_first[1:]:
                launch(lambda k=k: copy(self.block(0, 0), self.block(0, 0), self.y_pairs[k], to_y(k)))

        def cross(self, r):
            if r > 0:
                arrived(self.block(r, 0), self.y_pairs[r])
            for way in ways:
                launch(
                    lambda way=way: copy(
                        self.block(r, 0), self.block(r, 0), self.x_pairs[r, way], to_x(way)
                    )
                )

        def forward(self, r):
            for way in ways:
                arrived(self.block(r, -way), self.x_pairs[r, way])
            if xs > 2:
                way = side(r)
                launch(
                    lambda: copy(
                        self.block(r, -way), self.block(r, -way), self.far_pairs[r], to_x(way)
                    )
                )

        def share(self, r):
            if xs > 2:
                arrived(self.block(r, 2), self.far_pairs[r])

            def make():
                row = self.buf.at[c, mod(y - r, ys)]
                return copy(row, row, self.core_pairs[r], partner())

            launch(make)

        def wait(self, r):
            arrived(self.buf.at[1 - c, mod(y - r, ys)], self.core_pairs[r])

    factor_gather = Gather(factors)
    middle_gather = Gather(gathered)
    factor_gather.send()
    for k in range(1, zs):
        launch(lambda k=k: copy(wo_all.at[z], wo_all.at[z], wo_pairs[k - 1], to_z(k)))
    both = gate_up_ref[...].astype(F32)
    for n in range(2):
        gu_all[z, n * hidden : (n + 1) * hidden, :] = both[:, n, :].T.astype(BF16)
    down_rows = pl.ds(pl.multiple_of(z * down_cols, down_cols), down_cols)
    down_all[down_rows, :] = down_ref[...].astype(F32).T.astype(BF16)
    z_step(1)

    for n in range(2 * kv_heads):
        loads[n].wait()
    for n in range(kv_heads):
        values_all[n] = kv_all[kv_heads + n].astype(F32).T.astype(BF16)

    row = lax.broadcasted_iota(jnp.int32, (tokens, tokens), 0)
    bias_all[...] = jnp.where((row >= first) & (row <= column), 0.0, -1e30)

    def attend_one(h):
        kv = h // group
        for block in range(2):
            lo, hi = block * half, (block + 1) * half
            scores = lax.dot_general(
                kv_all[kv, :hi, :],
                q_all[h, lo:hi, :],
                (((1,), (1,)), ((), ())),
                preferred_element_type=F32,
            )
            scores = scores * HEAD ** (-0.5) + bias_all[:hi, lo:hi]
            top = jnp.max(scores, axis=0, keepdims=True)
            weights = jnp.exp(scores - top)
            total = jnp.sum(weights, axis=0, keepdims=True)
            mixed = dot(values_all[kv, :, :hi], weights.astype(BF16))
            attn_all[pl.ds(pl.multiple_of(h * HEAD, HEAD), HEAD), lo:hi] = (mixed / total).astype(BF16)

    def attend(n, carry):
        attend_one(2 * n)
        attend_one(2 * n + 1)
        return carry

    def attend_heads(lo, hi):
        for h in range(lo, hi):
            loads[2 * kv_heads + h].wait()
        lax.fori_loop(lo // 2, hi // 2, attend, 0)

    cut_one, cut_two = heads // 2, (3 * heads // 4) // 2 * 2
    attend_heads(0, cut_one)
    for r in near_first:
        factor_gather.cross(r)
    attend_heads(cut_one, cut_two)
    z_step(2)
    attend_heads(cut_two, heads)
    for r in near_first:
        factor_gather.forward(r)

    class AllReduce:
        def __init__(self, pair_buf, x_buf, xin, yin, back):
            self.bufs = (pair_buf, x_buf, xin, yin, back)
            self.pairs = [sems.take() for _ in range(2 + (xs - 1) + (ys - 1))]
            self.kind = pair_buf.dtype

        def start(self, value):
            pair_buf = self.bufs[0]
            pair_buf[0] = value[:, :half].astype(self.kind)
            pair_buf[1] = value[:, half:].astype(self.kind)
            launch(lambda: copy(pair_buf.at[1 - c], pair_buf.at[2], self.pairs[0], partner()))

        def cross(self):
            pair_buf, x_buf, xin, yin, back = self.bufs
            arrived(pair_buf.at[2], self.pairs[0])
            x_buf[0] = (pair_buf[c].astype(F32) + pair_buf[2].astype(F32)).astype(self.kind)
            for k in range(1, xs):
                launch(lambda k=k: copy(x_buf.at[0], xin.at[k - 1], self.pairs[k], to_x(k)))

        def along(self):
            pair_buf, x_buf, xin, yin, back = self.bufs
            total = x_buf[0].astype(F32)
            for k in range(1, xs):
                arrived(xin.at[k - 1], self.pairs[k])
                total = total + xin[k - 1].astype(F32)
            x_buf[1] = total.astype(self.kind)
            for k in range(1, ys):
                launch(
                    lambda k=k: copy(x_buf.at[1], yin.at[k - 1], self.pairs[xs - 1 + k], to_y(k))
                )

        def share(self):
            pair_buf, x_buf, xin, yin, back = self.bufs
            total = x_buf[1].astype(F32)
            for k in range(1, ys):
                arrived(yin.at[k - 1], self.pairs[xs - 1 + k])
                total = total + yin[k - 1].astype(F32)
            back[c] = total.astype(self.kind)
            launch(lambda: copy(back.at[c], back.at[c], self.pairs[-1], partner()))

        def result(self):
            back = self.bufs[4]
            arrived(back.at[1 - c], self.pairs[-1])
            return jnp.concatenate([back[0], back[1]], axis=1).astype(F32)

    def expand(rank):
        return jnp.concatenate([rank * members[p] for p in range(prompts)], axis=0).astype(BF16)

    def padded(rows, full):
        return jnp.concatenate([rows, jnp.zeros((full - rows.shape[0], tokens), BF16)], axis=0)

    out_reduce = AllReduce(rank_pair, rank_x, rank_xin, rank_yin, rank_back)
    gu_reduce = AllReduce(gu_pair, gu_x, gu_xin, gu_yin, gu_back)
    attn = attn_all[...]
    out_reduce.start(dot(ao_ref[...], attn) * owned)
    for k in range(1, zs):
        arrived(wo_all.at[places[zs - k]], wo_pairs[k - 1])
    weights = jnp.concatenate([wo_all[k] for k in range(zs)], axis=1)
    base = residual_ref[...].astype(F32) + dot(weights, attn)
    middle_ref[...] = base
    gathered[c, y, x] = base.astype(BF16)
    out_reduce.cross()

    middle_gather.send()
    for n in range(ys + 4):
        if n < ys:
            middle_gather.cross(near_first[n])
        if n == 2:
            out_reduce.along()
        if n == 4:
            z_step(3)
            for r in near_first:
                factor_gather.share(r)
        if 0 <= n - 2 < ys:
            middle_gather.forward(near_first[n - 2])
        if 0 <= n - 4 < ys:
            middle_gather.share(near_first[n - 4])
        if n == ys:
            z_step(4)
            out_reduce.share()
    for r in near_first:
        factor_gather.wait(r)
        middle_gather.wait(r)

    out_rank = padded(expand(ADAPTER_SCALE * out_reduce.result()), 128)
    middle_ref[...] += dot(factors[c, y, x, :, :128], out_rank)
    per_row = width // ys
    squares = jnp.zeros((8, tokens), F32)
    for row in range(ys):
        for core in range(CORES):
            block = factors[core, row].reshape(xs * CHUNK, 256)[:, :128]
            full = gathered[core, row].reshape(xs * CHUNK, tokens).astype(F32) + dot(block, out_rank)
            squares = squares + jnp.sum((full * full).reshape(-1, 8, tokens), axis=0)
            scaled = (full * block[:, gain_lane : gain_lane + 1].astype(F32)).astype(BF16)
            for col in range(xs):
                top = row * per_row + (col * CORES + core) * CHUNK
                normed[top : top + CHUNK, :] = scaled[col * CHUNK : (col + 1) * CHUNK]
    squares = jnp.sum(squares, axis=0, keepdims=True)
    inverse = lax.rsqrt(squares / width + EPS)

    for load in loads[2 * kv_heads + heads :]:
        load.wait()
    gu_reduce.start(dot(agu_ref[...], normed[...]) * (owned * inverse))
    for hop in range(5, ups + 1):
        z_step(hop)
    gu_reduce.cross()
    z_wait(max(ups, downs))
    weights = jnp.concatenate([gu_all[k] for k in range(zs)], axis=1)
    gu_reduce.along()
    joint = dot(weights, normed[...]) * inverse
    gu_reduce.share()
    gu_rank = gu_reduce.result()

    def hidden_correction(which, rank):
        rows = jnp.concatenate([bgu_ref[which, slot] for slot in slots], axis=0)
        return ADAPTER_SCALE * dot(rows.astype(F32).T.astype(BF16), expand(rank))

    gate = joint[:hidden] + hidden_correction(0, gu_rank[:ranks])
    up = joint[hidden:] + hidden_correction(1, gu_rank[ranks:])
    hidden_state = (jax.nn.gelu(gate, approximate=True) * up).astype(BF16)

    a_rows = jnp.concatenate([ad_ref[slot] for slot in slots], axis=0)
    shares = ADAPTER_SCALE * dot(a_rows, hidden_state)
    down_rank = jnp.concatenate(
        [shares[p * ranks : (p + 1) * ranks] * members[p] for p in range(prompts)], axis=0
    ).astype(BF16)
    source = jnp.concatenate([hidden_state, padded(down_rank, 128)], axis=0)
    share_pairs = [sems.take() for _ in range(ys)]
    near_pairs, away_pairs, on_pairs = [[sems.take() for _ in range(ys)] for _ in range(3)]
    last_pairs = [sems.take() for _ in range(ys)]
    for r in far_first:
        row = mod(y + r, ys)
        weights = down_all[pl.ds(pl.multiple_of(row * per_row, per_row), per_row), :]
        extra = jnp.concatenate(
            [factors[core, row, col, :, 128:] for col in range(xs) for core in range(CORES)], axis=0
        )
        block = dot(jnp.concatenate([weights, extra], axis=1), source).astype(BF16)
        for col in range(xs):
            for core in range(CORES):
                top = (col * CORES + core) * CHUNK
                partial[core, r, col] = block[top : top + CHUNK]
        launch(
            lambda r=r: copy(partial.at[1 - c, r], pair_in.at[r], share_pairs[r], partner())
        )

    def add_pair(r):
        arrived(pair_in.at[r], share_pairs[r])
        summed[r] = (partial[c, r].astype(F32) + pair_in[r].astype(F32)).astype(BF16)

    def begin(r):
        add_pair(r)
        way = side(r) if xs > 2 else 1
        if xs > 2:
            launch(
                lambda: copy(summed.at[r, mod(x + 2, xs)], away_in.at[r], away_pairs[r], to_x(way))
            )
        launch(
            lambda: copy(summed.at[r, mod(x - way, xs)], near_in.at[r], near_pairs[r], to_x(-way))
        )

    def carry_on(r):
        if xs > 2:
            way = side(r)
            arrived(away_in.at[r], away_pairs[r])
            total = summed[r, mod(x + way, xs)].astype(F32) + away_in[r].astype(F32)
            on_out[r] = total.astype(BF16)
            launch(lambda: copy(on_out.at[r], on_in.at[r], on_pairs[r], to_x(way)))

    def conclude(r):
        arrived(near_in.at[r], near_pairs[r])
        total = summed[r, x].astype(F32) + near_in[r].astype(F32)
        if xs > 2:
            arrived(on_in.at[r], on_pairs[r])
            total = total + on_in[r].astype(F32)
        last_out[r] = total.astype(BF16)
        if r > 0:
            launch(lambda: copy(last_out.at[r], last_in.at[r], last_pairs[r], to_y(r)))

    for n in range(ys + 4):
        if n < ys:
            begin(far_first[n])
        if 0 <= n - 2 < ys:
            carry_on(far_first[n - 2])
        if 0 <= n - 4 < ys:
            conclude(far_first[n - 4])
    total = middle_ref[...].astype(BF16).astype(F32) + last_out[0].astype(F32)
    for r in near_first[1:]:
        arrived(last_in.at[r], last_pairs[r])
        total = total + last_in[r].astype(F32)
    out_ref[...] = total.astype(BF16)
    for make in pending:
        make().wait_send()


def main_call(dims, args):
    zs, ys, xs = dims
    tokens, width = args[3].shape
    heads = width // HEAD
    kv_heads = args[4].shape[1] // (2 * HEAD)
    half = tokens // 2
    span, _, hidden = args[10].shape
    ranks = args[8].shape[0]

    def reduce_buffers(rows, kind):
        return [
            pltpu.VMEM((3, rows, half), kind),
            pltpu.VMEM((2, rows, half), kind),
            pltpu.VMEM((xs - 1, rows, half), kind),
            pltpu.VMEM((ys - 1, rows, half), kind),
            pltpu.VMEM((2, rows, half), kind),
        ]

    scratch = [
        pltpu.VMEM(args[11].shape, BF16),
        pltpu.VMEM(args[12].shape, BF16),
        pltpu.VMEM(args[14].shape, BF16),
        pltpu.VMEM((tokens, tokens), F32),
        pltpu.VMEM((heads, tokens, HEAD), BF16),
        pltpu.VMEM((2 * kv_heads, tokens, HEAD), BF16),
        pltpu.VMEM((kv_heads, HEAD, tokens), BF16),
        pltpu.VMEM((width, tokens), BF16),
        pltpu.VMEM((zs, CHUNK, span), BF16),
        pltpu.VMEM((zs, 2 * hidden, span), BF16),
        pltpu.VMEM((width, hidden), BF16),
        pltpu.VMEM((CORES, ys, xs, CHUNK, 256), BF16),
        pltpu.VMEM((CHUNK, tokens), F32),
        pltpu.VMEM((CORES, ys, xs, CHUNK, tokens), BF16),
        pltpu.VMEM((width, tokens), BF16),
        pltpu.VMEM((CORES, ys, xs, CHUNK, tokens), BF16),
        pltpu.VMEM((ys, xs, CHUNK, tokens), BF16),
        pltpu.VMEM((ys, xs, CHUNK, tokens), BF16),
    ]
    scratch += [pltpu.VMEM((ys, CHUNK, tokens), BF16)] * 6
    scratch += reduce_buffers(ranks, BF16)
    scratch += reduce_buffers(2 * ranks, BF16)
    scratch += [
        pltpu.SemaphoreType.DMA((heads + 2 * kv_heads + 3,)),
        pltpu.SemaphoreType.DMA((SEMAPHORES,)),
        pltpu.SemaphoreType.DMA((SEMAPHORES,)),
    ]
    smem = pl.BlockSpec(memory_space=pltpu.SMEM)
    vmem = pl.BlockSpec(memory_space=pltpu.VMEM)
    hbm = pl.BlockSpec(memory_space=pl.ANY)
    return pl.pallas_call(
        functools.partial(main_kernel, dims),
        out_shape=jax.ShapeDtypeStruct((CHUNK, tokens), BF16),
        in_specs=[smem] * 3 + [hbm] * 2 + [vmem] * 6 + [hbm] * 2 + [vmem, hbm, vmem],
        out_specs=vmem,
        scratch_shapes=scratch,
        compiler_params=pltpu.CompilerParams(
            collective_id=0, has_side_effects=True, vmem_limit_bytes=60 * 1024 * 1024
        ),
    )(*args)


def body(
    dims,
    residual_input,
    queries,
    key_value_pairs,
    prompt_length_list,
    prompt_adapter_index,
    adapter_position,
    output_matrix,
    output_factor_first,
    output_factor_second,
    norm_weight,
    gate_up_matrix,
    gate_up_factor_first,
    gate_up_factor_second,
    down_matrix,
    down_factor_first,
    down_factor_second,
):
    args = [
        prompt_length_list,
        prompt_adapter_index,
        adapter_position,
        queries,
        key_value_pairs,
        residual_input.T,
        norm_weight.reshape(1, -1),
        output_matrix.T,
        output_factor_first[0].T,
        output_factor_second.transpose(1, 2, 0),
        gate_up_matrix,
        gate_up_factor_first[0].T,
        gate_up_factor_second,
        down_matrix,
        down_factor_first.transpose(1, 2, 0),
        down_factor_second.transpose(1, 2, 0),
    ]
    return main_call(dims, args).T


def solution(mesh):
    placed = (
        P("req", "hid"),
        P("req", None),
        P("req", None),
        P("req", None),
        P("req", None),
        P(),
        P("req", "hid"),
        P("hid", None, None),
        P(None, None, "hid"),
        P("hid"),
        P("req", None, "hid"),
        P("hid", None, None),
        P(None, None, None, "hid"),
        P("hid", "req"),
        P("hid", None, None),
        P(None, None, "hid"),
    )
    dims = (mesh.shape["req"], mesh.shape["hid"] // (CORES * GRID_X), GRID_X)
    return jax.shard_map(
        functools.partial(body, dims),
        mesh=mesh,
        in_specs=placed,
        out_specs=P("req", "hid"),
        check_vma=False,
    )
```

```python
import functools

import jax
import jax.numpy as jnp
from jax import lax
from jax.experimental import pallas as pl
from jax.experimental.pallas import tpu as pltpu
from jax.sharding import PartitionSpec as P

HEADS = 8
KV_HEADS = 2
HEAD = 256
CHUNK = 32
CORES = 2
GRID_X = 4
ADAPTER_SCALE = 0.5
EPS = 1e-06

MESH = pl.DeviceIdType.MESH
F32 = jnp.float32
BF16 = jnp.bfloat16


def dot(a, b):
    return jnp.dot(a, b, preferred_element_type=F32)


def token_bounds(lengths_ref, count):
    bounds, total = [], 0
    for p in range(count):
        start = total
        total = total + lengths_ref[0, p]
        bounds.append((start, total))
    return bounds


class Sems:
    def __init__(self, send, recv, used=0):
        self.send, self.recv, self.used = send, recv, used

    def take(self):
        n = self.used
        self.used += 1
        return self.send.at[n], self.recv.at[n]


SEMAPHORES = 400


def main_kernel(
    dims,
    lengths_ref,
    adapters_ref,
    places_ref,
    queries_ref,
    pairs_ref,
    residual_ref,
    gain_ref,
    wo_ref,
    ao_ref,
    bo_ref,
    gate_up_ref,
    agu_hbm,
    bgu_hbm,
    down_ref,
    ad_hbm,
    bd_ref,
    out_ref,
    agu_ref,
    bgu_ref,
    ad_ref,
    bias_all,
    joint_all,
    q_all,
    kv_all,
    values_all,
    attn_all,
    wo_all,
    gu_all,
    down_all,
    factors,
    middle_ref,
    gathered,
    normed,
    partial,
    pair_in,
    summed,
    near_in,
    away_in,
    on_out,
    on_in,
    last_out,
    last_in,
    rank_pair,
    rank_x,
    rank_xin,
    rank_yin,
    rank_back,
    gu_pair,
    gu_x,
    gu_xin,
    gu_yin,
    gu_back,
    local_sems,
    send_sems,
    recv_sems,
):
    zs, ys, xs = dims
    heads, tokens, _ = q_all.shape
    kv_heads = values_all.shape[0]
    group = heads // kv_heads
    half = tokens // 2
    width = attn_all.shape[0]
    prompts = lengths_ref.shape[1]
    ranks = ao_ref.shape[0]
    z = lax.axis_index("req")
    me = lax.axis_index("hid")
    c = lax.rem(me, CORES)
    x = lax.rem(me // CORES, xs)
    y = me // (CORES * xs)
    sems = Sems(send_sems, recv_sems)
    pending = []

    def at(yy, xx, cc):
        return (z, yy * (xs * CORES) + xx * CORES + cc)

    def mod(value, size):
        return lax.rem(value + size, size)

    def partner():
        return at(y, x, 1 - c)

    def to_x(k):
        return at(y, mod(x + k, xs), c)

    def to_y(k):
        return at(mod(y + k, ys), x, c)

    def to_z(k):
        return (mod(z + k, zs), me)

    def copy(src, dst, pair, device):
        return pltpu.make_async_remote_copy(
            src_ref=src,
            dst_ref=dst,
            send_sem=pair[0],
            recv_sem=pair[1],
            device_id=device,
            device_id_type=MESH,
        )

    def arrived(dst, pair):
        copy(dst, dst, pair, partner()).wait_recv()

    def launch(make):
        make().start()
        pending.append(make)

    loads = []
    for n in range(2 * kv_heads):
        loads.append(
            pltpu.make_async_copy(
                pairs_ref.at[:, n * HEAD : (n + 1) * HEAD], kv_all.at[n], local_sems.at[n]
            )
        )
    for h in range(heads):
        loads.append(
            pltpu.make_async_copy(
                queries_ref.at[:, h * HEAD : (h + 1) * HEAD],
                q_all.at[h],
                local_sems.at[2 * kv_heads + h],
            )
        )
    for n, (src, dst) in enumerate(((agu_hbm, agu_ref), (bgu_hbm, bgu_ref), (ad_hbm, ad_ref))):
        loads.append(pltpu.make_async_copy(src, dst, local_sems.at[2 * kv_heads + heads + n]))
    for load in loads:
        load.start()

    barrier = pltpu.get_barrier_semaphore()
    peers = [partner()]
    peers += [to_x(k) for k in range(1, xs)]
    peers += [to_y(k) for k in range(1, ys)]
    peers += [to_z(k) for k in range(1, zs)]
    for peer in peers:
        pl.semaphore_signal(barrier, inc=1, device_id=peer, device_id_type=MESH)

    wo_all[z] = wo_ref[...]
    hidden = gate_up_ref.shape[2]
    down_cols = down_ref.shape[1]

    column = lax.broadcasted_iota(jnp.int32, (1, tokens), 1)
    adapters = bo_ref.shape[2]
    lane = lax.broadcasted_iota(jnp.int32, (1, 128), 1)
    slots, members = [], []
    owned = jnp.zeros((1, tokens), F32)
    first = jnp.zeros((1, tokens), jnp.int32)
    slot_lane = jnp.full((1, 128), -1, jnp.int32)
    total = 0
    for p in range(prompts):
        start = total
        total = total + lengths_ref[0, p]
        slot = places_ref[adapters_ref[0, p]]
        inside = (column >= start) & (column < total)
        slots.append(slot)
        members.append(inside.astype(F32))
        owned = owned + jnp.where(inside, jnp.where(slot == me, 1.0, 0.0), 0.0)
        first = jnp.where(inside, start, first)
        slot_lane = jnp.where(lane // ranks == p, slot, slot_lane)

    adapter_row = lax.broadcasted_iota(jnp.int32, (adapters, 128), 0)
    out_factor = jnp.zeros((CHUNK, 128), F32)
    down_factor = jnp.zeros((CHUNK, 128), F32)
    for r in range(ranks):
        pick = ((adapter_row == slot_lane) & (lax.rem(lane, ranks) == r)).astype(BF16)
        out_factor = out_factor + dot(bo_ref[r], pick)
        down_factor = down_factor + dot(bd_ref[r], pick)
    diagonal = lax.broadcasted_iota(jnp.int32, (CHUNK, CHUNK), 0) == lax.broadcasted_iota(
        jnp.int32, (CHUNK, CHUNK), 1
    )
    gain = jnp.sum(jnp.where(diagonal, gain_ref[...].astype(F32), 0.0), axis=1, keepdims=True)
    gain_lane = prompts * ranks
    out_factor = jnp.where(lane == gain_lane, gain, out_factor)
    factors[c, y, x] = jnp.concatenate([out_factor, down_factor], axis=1).astype(BF16)

    pl.semaphore_wait(barrier, len(peers))

    places = [mod(z + k, zs) for k in range(zs)]
    wo_pairs = [sems.take() for _ in range(zs - 1)]
    ups, downs = zs // 2, (zs - 1) // 2
    z_pairs = {}
    for way, hops in ((1, ups), (-1, downs)):
        for hop in range(1, hops + 1):
            z_pairs[way, hop] = (sems.take(), sems.take())

    def z_slot(way, hop):
        return mod(z - way * hop, zs)

    def z_block(way, hop):
        slot = z_slot(way, hop)
        return (
            gu_all.at[slot],
            down_all.at[pl.ds(pl.multiple_of(slot * down_cols, down_cols), down_cols), :],
        )

    def z_wait(hop):
        for way, hops in ((1, ups), (-1, downs)):
            if 1 <= hop <= hops:
                for n, block in enumerate(z_block(way, hop)):
                    arrived(block, z_pairs[way, hop][n])

    def z_step(hop):
        z_wait(hop - 1)
        for way, hops in ((1, ups), (-1, downs)):
            if hop <= hops:
                for n in range(2):

                    def make(way=way, n=n):
                        block = z_block(way, hop - 1)[n]
                        return copy(block, block, z_pairs[way, hop][n], to_z(way))

                    launch(make)

    near_first = sorted(range(ys), key=lambda k: min(k, ys - k))
    far_first = near_first[::-1]
    ways = (1, -1) if xs > 2 else (1,)

    def side(r):
        return 1 if r % 2 == 0 else -1

    class Gather:
        def __init__(self, buf):
            self.buf = buf
            self.y_pairs = [None] + [sems.take() for _ in range(1, ys)]
            self.x_pairs = {(r, way): sems.take() for r in range(ys) for way in ways}
            self.far_pairs = [sems.take() for _ in range(ys)]
            self.core_pairs = [sems.take() for _ in range(ys)]

        def block(self, r, k):
            return self.buf.at[c, mod(y - r, ys), mod(x + k, xs)]

        def send(self):
            for k in near_first[1:]:
                launch(lambda k=k: copy(self.block(0, 0), self.block(0, 0), self.y_pairs[k], to_y(k)))

        def cross(self, r):
            if r > 0:
                arrived(self.block(r, 0), self.y_pairs[r])
            for way in ways:
                launch(
                    lambda way=way: copy(
                        self.block(r, 0), self.block(r, 0), self.x_pairs[r, way], to_x(way)
                    )
                )

        def forward(self, r):
            for way in ways:
                arrived(self.block(r, -way), self.x_pairs[r, way])
            if xs > 2:
                way = side(r)
                launch(
                    lambda: copy(
                        self.block(r, -way), self.block(r, -way), self.far_pairs[r], to_x(way)
                    )
                )

        def share(self, r):
            if xs > 2:
                arrived(self.block(r, 2), self.far_pairs[r])

            def make():
                row = self.buf.at[c, mod(y - r, ys)]
                return copy(row, row, self.core_pairs[r], partner())

            launch(make)

        def wait(self, r):
            arrived(self.buf.at[1 - c, mod(y - r, ys)], self.core_pairs[r])

    factor_gather = Gather(factors)
    middle_gather = Gather(gathered)
    factor_gather.send()
    for k in range(1, zs):
        launch(lambda k=k: copy(wo_all.at[z], wo_all.at[z], wo_pairs[k - 1], to_z(k)))
    both = gate_up_ref[...].astype(F32)
    for n in range(2):
        gu_all[z, n * hidden : (n + 1) * hidden, :] = both[:, n, :].T.astype(BF16)
    down_rows = pl.ds(pl.multiple_of(z * down_cols, down_cols), down_cols)
    down_all[down_rows, :] = down_ref[...].astype(F32).T.astype(BF16)
    z_step(1)

    for n in range(2 * kv_heads):
        loads[n].wait()
    for n in range(kv_heads):
        values_all[n] = kv_all[kv_heads + n].astype(F32).T.astype(BF16)

    row = lax.broadcasted_iota(jnp.int32, (tokens, tokens), 0)
    bias_all[...] = jnp.where((row >= first) & (row <= column), 0.0, -1e30)

    def attend_one(h):
        kv = h // group
        for block in range(2):
            lo, hi = block * half, (block + 1) * half
            scores = lax.dot_general(
                kv_all[kv, :hi, :],
                q_all[h, lo:hi, :],
                (((1,), (1,)), ((), ())),
                preferred_element_type=F32,
            )
            scores = scores * HEAD ** (-0.5) + bias_all[:hi, lo:hi]
            top = jnp.max(scores, axis=0, keepdims=True)
            weights = jnp.exp(scores - top)
            total = jnp.sum(weights, axis=0, keepdims=True)
            mixed = dot(values_all[kv, :, :hi], weights.astype(BF16))
            attn_all[pl.ds(pl.multiple_of(h * HEAD, HEAD), HEAD), lo:hi] = (mixed / total).astype(BF16)

    def attend(n, carry):
        for k in range(4):
            attend_one(4 * n + k)
        return carry

    def attend_heads(lo, hi):
        for h in range(lo, hi):
            loads[2 * kv_heads + h].wait()
        lax.fori_loop(lo // 4, hi // 4, attend, 0)

    cut_one, cut_two = heads // 2, heads
    attend_heads(0, cut_one)
    for r in near_first:
        factor_gather.cross(r)
    attend_heads(cut_one, cut_two)
    z_step(2)
    attend_heads(cut_two, heads)
    for r in near_first:
        factor_gather.forward(r)

    class AllReduce:
        def __init__(self, pair_buf, x_buf, xin, yin, back):
            self.bufs = (pair_buf, x_buf, xin, yin, back)
            self.pairs = [sems.take() for _ in range(2 + (xs - 1) + (ys - 1))]
            self.kind = pair_buf.dtype

        def start(self, value):
            pair_buf = self.bufs[0]
            pair_buf[0] = value[:, :half].astype(self.kind)
            pair_buf[1] = value[:, half:].astype(self.kind)
            launch(lambda: copy(pair_buf.at[1 - c], pair_buf.at[2], self.pairs[0], partner()))

        def cross(self):
            pair_buf, x_buf, xin, yin, back = self.bufs
            arrived(pair_buf.at[2], self.pairs[0])
            x_buf[0] = (pair_buf[c].astype(F32) + pair_buf[2].astype(F32)).astype(self.kind)
            for k in range(1, xs):
                launch(lambda k=k: copy(x_buf.at[0], xin.at[k - 1], self.pairs[k], to_x(k)))

        def along(self):
            pair_buf, x_buf, xin, yin, back = self.bufs
            total = x_buf[0].astype(F32)
            for k in range(1, xs):
                arrived(xin.at[k - 1], self.pairs[k])
                total = total + xin[k - 1].astype(F32)
            x_buf[1] = total.astype(self.kind)
            for k in range(1, ys):
                launch(
                    lambda k=k: copy(x_buf.at[1], yin.at[k - 1], self.pairs[xs - 1 + k], to_y(k))
                )

        def share(self):
            pair_buf, x_buf, xin, yin, back = self.bufs
            total = x_buf[1].astype(F32)
            for k in range(1, ys):
                arrived(yin.at[k - 1], self.pairs[xs - 1 + k])
                total = total + yin[k - 1].astype(F32)
            back[c] = total.astype(self.kind)
            launch(lambda: copy(back.at[c], back.at[c], self.pairs[-1], partner()))

        def result(self):
            back = self.bufs[4]
            arrived(back.at[1 - c], self.pairs[-1])
            return jnp.concatenate([back[0], back[1]], axis=1).astype(F32)

    def expand(rank):
        return jnp.concatenate([rank * members[p] for p in range(prompts)], axis=0).astype(BF16)

    def padded(rows, full):
        return jnp.concatenate([rows, jnp.zeros((full - rows.shape[0], tokens), BF16)], axis=0)

    out_reduce = AllReduce(rank_pair, rank_x, rank_xin, rank_yin, rank_back)
    gu_reduce = AllReduce(gu_pair, gu_x, gu_xin, gu_yin, gu_back)
    attn = attn_all[...]
    out_reduce.start(dot(ao_ref[...], attn) * owned)
    for k in range(1, zs):
        arrived(wo_all.at[places[zs - k]], wo_pairs[k - 1])
    weights = jnp.concatenate([wo_all[k] for k in range(zs)], axis=1)
    base = residual_ref[...].astype(F32) + dot(weights, attn)
    middle_ref[...] = base
    gathered[c, y, x] = base.astype(BF16)
    out_reduce.cross()

    middle_gather.send()
    for n in range(ys + 4):
        if n < ys:
            middle_gather.cross(near_first[n])
        if n == 2:
            out_reduce.along()
        if n == 4:
            z_step(3)
            for r in near_first:
                factor_gather.share(r)
        if 0 <= n - 2 < ys:
            middle_gather.forward(near_first[n - 2])
        if 0 <= n - 4 < ys:
            middle_gather.share(near_first[n - 4])
        if n == ys:
            z_step(4)
            out_reduce.share()
    for r in near_first:
        factor_gather.wait(r)

    out_rank = padded(expand(ADAPTER_SCALE * out_reduce.result()), 128)
    middle_ref[...] += dot(factors[c, y, x, :, :128], out_rank)
    per_row = width // ys
    squares = jnp.zeros((8, tokens), F32)
    for r in near_first:
        middle_gather.wait(r)
        row = mod(y - r, ys)
        for core in range(CORES):
            block = factors[core, row].reshape(xs * CHUNK, 256)[:, :128]
            full = gathered[core, row].reshape(xs * CHUNK, tokens).astype(F32) + dot(block, out_rank)
            squares = squares + jnp.sum((full * full).reshape(-1, 8, tokens), axis=0)
            scaled = (full * block[:, gain_lane : gain_lane + 1].astype(F32)).astype(BF16)
            for col in range(xs):
                top = pl.multiple_of(row * per_row + (col * CORES + core) * CHUNK, CHUNK)
                normed[pl.ds(top, CHUNK), :] = scaled[col * CHUNK : (col + 1) * CHUNK]
    squares = jnp.sum(squares, axis=0, keepdims=True)
    inverse = lax.rsqrt(squares / width + EPS)

    for load in loads[2 * kv_heads + heads :]:
        load.wait()
    gu_reduce.start(dot(agu_ref[...], normed[...]) * (owned * inverse))
    for hop in range(5, ups + 1):
        z_step(hop)
    gu_reduce.cross()
    z_wait(max(ups, downs))
    weights = jnp.concatenate([gu_all[k] for k in range(zs)], axis=1)
    gu_reduce.along()
    joint_all[...] = dot(weights, normed[...]) * inverse
    hidden_factors = []
    for which in range(2):
        rows = jnp.concatenate([bgu_ref[which, slot] for slot in slots], axis=0)
        hidden_factors.append(rows.astype(F32).T.astype(BF16))
    a_rows = jnp.concatenate([ad_ref[slot] for slot in slots], axis=0)
    gu_reduce.share()
    gu_rank = gu_reduce.result()

    def hidden_correction(which, rank):
        return ADAPTER_SCALE * dot(hidden_factors[which], expand(rank))

    gate = joint_all[:hidden] + hidden_correction(0, gu_rank[:ranks])
    up = joint_all[hidden:] + hidden_correction(1, gu_rank[ranks:])
    hidden_state = (jax.nn.gelu(gate, approximate=True) * up).astype(BF16)

    shares = ADAPTER_SCALE * dot(a_rows, hidden_state)
    down_rank = jnp.concatenate(
        [shares[p * ranks : (p + 1) * ranks] * members[p] for p in range(prompts)], axis=0
    ).astype(BF16)
    source = jnp.concatenate([hidden_state, padded(down_rank, 128)], axis=0)
    share_pairs = [sems.take() for _ in range(ys)]
    near_pairs, away_pairs, on_pairs = [[sems.take() for _ in range(ys)] for _ in range(3)]
    last_pairs = [sems.take() for _ in range(ys)]
    for r in far_first:
        row = mod(y + r, ys)
        weights = down_all[pl.ds(pl.multiple_of(row * per_row, per_row), per_row), :]
        extra = jnp.concatenate(
            [factors[core, row, col, :, 128:] for col in range(xs) for core in range(CORES)], axis=0
        )
        block = dot(jnp.concatenate([weights, extra], axis=1), source).astype(BF16)
        for col in range(xs):
            for core in range(CORES):
                top = (col * CORES + core) * CHUNK
                partial[core, r, col] = block[top : top + CHUNK]
        launch(
            lambda r=r: copy(partial.at[1 - c, r], pair_in.at[r], share_pairs[r], partner())
        )

    def add_pair(r):
        arrived(pair_in.at[r], share_pairs[r])
        summed[r] = (partial[c, r].astype(F32) + pair_in[r].astype(F32)).astype(BF16)

    def begin(r):
        add_pair(r)
        way = side(r) if xs > 2 else 1
        if xs > 2:
            launch(
                lambda: copy(summed.at[r, mod(x + 2, xs)], away_in.at[r], away_pairs[r], to_x(way))
            )
        launch(
            lambda: copy(summed.at[r, mod(x - way, xs)], near_in.at[r], near_pairs[r], to_x(-way))
        )

    def carry_on(r):
        if xs > 2:
            way = side(r)
            arrived(away_in.at[r], away_pairs[r])
            total = summed[r, mod(x + way, xs)].astype(F32) + away_in[r].astype(F32)
            on_out[r] = total.astype(BF16)
            launch(lambda: copy(on_out.at[r], on_in.at[r], on_pairs[r], to_x(way)))

    def conclude(r):
        arrived(near_in.at[r], near_pairs[r])
        total = summed[r, x].astype(F32) + near_in[r].astype(F32)
        if xs > 2:
            arrived(on_in.at[r], on_pairs[r])
            total = total + on_in[r].astype(F32)
        last_out[r] = total.astype(BF16)
        if r > 0:
            launch(lambda: copy(last_out.at[r], last_in.at[r], last_pairs[r], to_y(r)))

    for n in range(ys + 4):
        if n < ys:
            begin(far_first[n])
        if 0 <= n - 2 < ys:
            carry_on(far_first[n - 2])
        if 0 <= n - 4 < ys:
            conclude(far_first[n - 4])
    total = middle_ref[...].astype(BF16).astype(F32) + last_out[0].astype(F32)
    for r in near_first[1:]:
        arrived(last_in.at[r], last_pairs[r])
        total = total + last_in[r].astype(F32)
    out_ref[...] = total.astype(BF16)
    for make in pending:
        make().wait_send()


def main_call(dims, args):
    zs, ys, xs = dims
    tokens, width = args[3].shape
    heads = width // HEAD
    kv_heads = args[4].shape[1] // (2 * HEAD)
    half = tokens // 2
    span, _, hidden = args[10].shape
    ranks = args[8].shape[0]

    def reduce_buffers(rows, kind):
        return [
            pltpu.VMEM((3, rows, half), kind),
            pltpu.VMEM((2, rows, half), kind),
            pltpu.VMEM((xs - 1, rows, half), kind),
            pltpu.VMEM((ys - 1, rows, half), kind),
            pltpu.VMEM((2, rows, half), kind),
        ]

    scratch = [
        pltpu.VMEM(args[11].shape, BF16),
        pltpu.VMEM(args[12].shape, BF16),
        pltpu.VMEM(args[14].shape, BF16),
        pltpu.VMEM((tokens, tokens), F32),
        pltpu.VMEM((2 * hidden, tokens), F32),
        pltpu.VMEM((heads, tokens, HEAD), BF16),
        pltpu.VMEM((2 * kv_heads, tokens, HEAD), BF16),
        pltpu.VMEM((kv_heads, HEAD, tokens), BF16),
        pltpu.VMEM((width, tokens), BF16),
        pltpu.VMEM((zs, CHUNK, span), BF16),
        pltpu.VMEM((zs, 2 * hidden, span), BF16),
        pltpu.VMEM((width, hidden), BF16),
        pltpu.VMEM((CORES, ys, xs, CHUNK, 256), BF16),
        pltpu.VMEM((CHUNK, tokens), F32),
        pltpu.VMEM((CORES, ys, xs, CHUNK, tokens), BF16),
        pltpu.VMEM((width, tokens), BF16),
        pltpu.VMEM((CORES, ys, xs, CHUNK, tokens), BF16),
        pltpu.VMEM((ys, xs, CHUNK, tokens), BF16),
        pltpu.VMEM((ys, xs, CHUNK, tokens), BF16),
    ]
    scratch += [pltpu.VMEM((ys, CHUNK, tokens), BF16)] * 6
    scratch += reduce_buffers(ranks, BF16)
    scratch += reduce_buffers(2 * ranks, BF16)
    scratch += [
        pltpu.SemaphoreType.DMA((heads + 2 * kv_heads + 3,)),
        pltpu.SemaphoreType.DMA((SEMAPHORES,)),
        pltpu.SemaphoreType.DMA((SEMAPHORES,)),
    ]
    smem = pl.BlockSpec(memory_space=pltpu.SMEM)
    vmem = pl.BlockSpec(memory_space=pltpu.VMEM)
    hbm = pl.BlockSpec(memory_space=pl.ANY)
    return pl.pallas_call(
        functools.partial(main_kernel, dims),
        out_shape=jax.ShapeDtypeStruct((CHUNK, tokens), BF16),
        in_specs=[smem] * 3 + [hbm] * 2 + [vmem] * 6 + [hbm] * 2 + [vmem, hbm, vmem],
        out_specs=vmem,
        scratch_shapes=scratch,
        compiler_params=pltpu.CompilerParams(
            collective_id=0, has_side_effects=True, vmem_limit_bytes=60 * 1024 * 1024
        ),
    )(*args)


def body(
    dims,
    residual_input,
    queries,
    key_value_pairs,
    prompt_length_list,
    prompt_adapter_index,
    adapter_position,
    output_matrix,
    output_factor_first,
    output_factor_second,
    norm_weight,
    gate_up_matrix,
    gate_up_factor_first,
    gate_up_factor_second,
    down_matrix,
    down_factor_first,
    down_factor_second,
):
    args = [
        prompt_length_list,
        prompt_adapter_index,
        adapter_position,
        queries,
        key_value_pairs,
        residual_input.T,
        norm_weight.reshape(1, -1),
        output_matrix.T,
        output_factor_first[0].T,
        output_factor_second.transpose(1, 2, 0),
        gate_up_matrix,
        gate_up_factor_first[0].T,
        gate_up_factor_second,
        down_matrix,
        down_factor_first.transpose(1, 2, 0),
        down_factor_second.transpose(1, 2, 0),
    ]
    return main_call(dims, args).T


def solution(mesh):
    placed = (
        P("req", "hid"),
        P("req", None),
        P("req", None),
        P("req", None),
        P("req", None),
        P(),
        P("req", "hid"),
        P("hid", None, None),
        P(None, None, "hid"),
        P("hid"),
        P("req", None, "hid"),
        P("hid", None, None),
        P(None, None, None, "hid"),
        P("hid", "req"),
        P("hid", None, None),
        P(None, None, "hid"),
    )
    dims = (mesh.shape["req"], mesh.shape["hid"] // (CORES * GRID_X), GRID_X)
    return jax.shard_map(
        functools.partial(body, dims),
        mesh=mesh,
        in_specs=placed,
        out_specs=P("req", "hid"),
        check_vma=False,
    )
```

```python
import functools

import jax
import jax.numpy as jnp
from jax import lax
from jax.experimental import pallas as pl
from jax.experimental.pallas import tpu as pltpu
from jax.sharding import PartitionSpec as P

HEADS = 8
KV_HEADS = 2
HEAD = 256
CHUNK = 32
CORES = 2
GRID_X = 4
ADAPTER_SCALE = 0.5
EPS = 1e-06

MESH = pl.DeviceIdType.MESH
F32 = jnp.float32
BF16 = jnp.bfloat16


def dot(a, b):
    return jnp.dot(a, b, preferred_element_type=F32)


def token_bounds(lengths_ref, count):
    bounds, total = [], 0
    for p in range(count):
        start = total
        total = total + lengths_ref[0, p]
        bounds.append((start, total))
    return bounds


class Sems:
    def __init__(self, send, recv, used=0):
        self.send, self.recv, self.used = send, recv, used

    def take(self):
        n = self.used
        self.used += 1
        return self.send.at[n], self.recv.at[n]


SEMAPHORES = 400


def main_kernel(
    dims,
    lengths_ref,
    adapters_ref,
    places_ref,
    queries_ref,
    pairs_ref,
    residual_ref,
    gain_ref,
    wo_ref,
    ao_ref,
    bo_ref,
    gate_up_ref,
    agu_hbm,
    bgu_hbm,
    down_ref,
    ad_hbm,
    bd_ref,
    out_ref,
    agu_ref,
    bgu_ref,
    ad_ref,
    bias_all,
    joint_all,
    q_all,
    kv_all,
    values_all,
    attn_all,
    wo_all,
    gu_all,
    down_all,
    factors,
    middle_ref,
    gathered,
    normed,
    partial,
    pair_in,
    summed,
    near_in,
    away_in,
    on_out,
    on_in,
    last_out,
    last_in,
    rank_pair,
    rank_x,
    rank_xin,
    rank_yin,
    rank_back,
    gu_pair,
    gu_x,
    gu_xin,
    gu_yin,
    gu_back,
    local_sems,
    send_sems,
    recv_sems,
):
    zs, ys, xs = dims
    heads, tokens, _ = q_all.shape
    kv_heads = values_all.shape[0]
    group = heads // kv_heads
    half = tokens // 2
    width = attn_all.shape[0]
    prompts = lengths_ref.shape[1]
    ranks = ao_ref.shape[0]
    z = lax.axis_index("req")
    me = lax.axis_index("hid")
    c = lax.rem(me, CORES)
    x = lax.rem(me // CORES, xs)
    y = me // (CORES * xs)
    sems = Sems(send_sems, recv_sems)
    pending = []

    def at(yy, xx, cc):
        return (z, yy * (xs * CORES) + xx * CORES + cc)

    def mod(value, size):
        return lax.rem(value + size, size)

    def partner():
        return at(y, x, 1 - c)

    def to_x(k):
        return at(y, mod(x + k, xs), c)

    def to_y(k):
        return at(mod(y + k, ys), x, c)

    def to_z(k):
        return (mod(z + k, zs), me)

    def copy(src, dst, pair, device):
        return pltpu.make_async_remote_copy(
            src_ref=src,
            dst_ref=dst,
            send_sem=pair[0],
            recv_sem=pair[1],
            device_id=device,
            device_id_type=MESH,
        )

    def arrived(dst, pair):
        copy(dst, dst, pair, partner()).wait_recv()

    def launch(make):
        make().start()
        pending.append(make)

    loads = []
    for n in range(2 * kv_heads):
        loads.append(
            pltpu.make_async_copy(
                pairs_ref.at[:, n * HEAD : (n + 1) * HEAD], kv_all.at[n], local_sems.at[n]
            )
        )
    for h in range(heads):
        loads.append(
            pltpu.make_async_copy(
                queries_ref.at[:, h * HEAD : (h + 1) * HEAD],
                q_all.at[h],
                local_sems.at[2 * kv_heads + h],
            )
        )
    for n, (src, dst) in enumerate(((agu_hbm, agu_ref), (bgu_hbm, bgu_ref), (ad_hbm, ad_ref))):
        loads.append(pltpu.make_async_copy(src, dst, local_sems.at[2 * kv_heads + heads + n]))
    for load in loads:
        load.start()

    barrier = pltpu.get_barrier_semaphore()
    peers = [partner()]
    peers += [to_x(k) for k in range(1, xs)]
    peers += [to_y(k) for k in range(1, ys)]
    peers += [to_z(k) for k in range(1, zs)]
    for peer in peers:
        pl.semaphore_signal(barrier, inc=1, device_id=peer, device_id_type=MESH)

    wo_all[z] = wo_ref[...]
    hidden = gate_up_ref.shape[2]
    down_cols = down_ref.shape[1]

    column = lax.broadcasted_iota(jnp.int32, (1, tokens), 1)
    adapters = bo_ref.shape[2]
    lane = lax.broadcasted_iota(jnp.int32, (1, 128), 1)
    slots, members = [], []
    owned = jnp.zeros((1, tokens), F32)
    first = jnp.zeros((1, tokens), jnp.int32)
    slot_lane = jnp.full((1, 128), -1, jnp.int32)
    total = 0
    for p in range(prompts):
        start = total
        total = total + lengths_ref[0, p]
        slot = places_ref[adapters_ref[0, p]]
        inside = (column >= start) & (column < total)
        slots.append(slot)
        members.append(inside.astype(F32))
        owned = owned + jnp.where(inside, jnp.where(slot == me, 1.0, 0.0), 0.0)
        first = jnp.where(inside, start, first)
        slot_lane = jnp.where(lane // ranks == p, slot, slot_lane)

    adapter_row = lax.broadcasted_iota(jnp.int32, (adapters, 128), 0)
    out_factor = jnp.zeros((CHUNK, 128), F32)
    down_factor = jnp.zeros((CHUNK, 128), F32)
    for r in range(ranks):
        pick = ((adapter_row == slot_lane) & (lax.rem(lane, ranks) == r)).astype(BF16)
        out_factor = out_factor + dot(bo_ref[r], pick)
        down_factor = down_factor + dot(bd_ref[r], pick)
    diagonal = lax.broadcasted_iota(jnp.int32, (CHUNK, CHUNK), 0) == lax.broadcasted_iota(
        jnp.int32, (CHUNK, CHUNK), 1
    )
    gain = jnp.sum(jnp.where(diagonal, gain_ref[...].astype(F32), 0.0), axis=1, keepdims=True)
    gain_lane = prompts * ranks
    out_factor = jnp.where(lane == gain_lane, gain, out_factor)
    factors[c, y, x] = jnp.concatenate([out_factor, down_factor], axis=1).astype(BF16)

    pl.semaphore_wait(barrier, len(peers))

    places = [mod(z + k, zs) for k in range(zs)]
    wo_pairs = [sems.take() for _ in range(zs - 1)]
    ups, downs = zs // 2, (zs - 1) // 2
    z_pairs = {}
    for way, hops in ((1, ups), (-1, downs)):
        for hop in range(1, hops + 1):
            z_pairs[way, hop] = (sems.take(), sems.take())

    def z_slot(way, hop):
        return mod(z - way * hop, zs)

    def z_block(way, hop):
        slot = z_slot(way, hop)
        return (
            gu_all.at[slot],
            down_all.at[pl.ds(pl.multiple_of(slot * down_cols, down_cols), down_cols), :],
        )

    def z_wait(hop):
        for way, hops in ((1, ups), (-1, downs)):
            if 1 <= hop <= hops:
                for n, block in enumerate(z_block(way, hop)):
                    arrived(block, z_pairs[way, hop][n])

    def z_step(hop):
        z_wait(hop - 1)
        for way, hops in ((1, ups), (-1, downs)):
            if hop <= hops:
                for n in range(2):

                    def make(way=way, n=n):
                        block = z_block(way, hop - 1)[n]
                        return copy(block, block, z_pairs[way, hop][n], to_z(way))

                    launch(make)

    near_first = sorted(range(ys), key=lambda k: min(k, ys - k))
    far_first = near_first[::-1]
    ways = (1, -1) if xs > 2 else (1,)

    def side(r):
        return 1 if r % 2 == 0 else -1

    class Gather:
        def __init__(self, buf):
            self.buf = buf
            self.y_pairs = [None] + [sems.take() for _ in range(1, ys)]
            self.x_pairs = {(r, way): sems.take() for r in range(ys) for way in ways}
            self.far_pairs = [sems.take() for _ in range(ys)]
            self.core_pairs = [sems.take() for _ in range(ys)]

        def block(self, r, k):
            return self.buf.at[c, mod(y - r, ys), mod(x + k, xs)]

        def send(self):
            for k in near_first[1:]:
                launch(lambda k=k: copy(self.block(0, 0), self.block(0, 0), self.y_pairs[k], to_y(k)))

        def cross(self, r):
            if r > 0:
                arrived(self.block(r, 0), self.y_pairs[r])
            for way in ways:
                launch(
                    lambda way=way: copy(
                        self.block(r, 0), self.block(r, 0), self.x_pairs[r, way], to_x(way)
                    )
                )

        def forward(self, r):
            for way in ways:
                arrived(self.block(r, -way), self.x_pairs[r, way])
            if xs > 2:
                way = side(r)
                launch(
                    lambda: copy(
                        self.block(r, -way), self.block(r, -way), self.far_pairs[r], to_x(way)
                    )
                )

        def share(self, r):
            if xs > 2:
                arrived(self.block(r, 2), self.far_pairs[r])

            def make():
                row = self.buf.at[c, mod(y - r, ys)]
                return copy(row, row, self.core_pairs[r], partner())

            launch(make)

        def wait(self, r):
            arrived(self.buf.at[1 - c, mod(y - r, ys)], self.core_pairs[r])

    factor_gather = Gather(factors)
    middle_gather = Gather(gathered)
    factor_gather.send()
    for k in range(1, zs):
        launch(lambda k=k: copy(wo_all.at[z], wo_all.at[z], wo_pairs[k - 1], to_z(k)))
    both = gate_up_ref[...].astype(F32)
    for n in range(2):
        gu_all[z, n * hidden : (n + 1) * hidden, :] = both[:, n, :].T.astype(BF16)
    down_rows = pl.ds(pl.multiple_of(z * down_cols, down_cols), down_cols)
    down_all[down_rows, :] = down_ref[...].astype(F32).T.astype(BF16)
    z_step(1)

    for n in range(2 * kv_heads):
        loads[n].wait()
    for n in range(kv_heads):
        values_all[n] = kv_all[kv_heads + n].astype(F32).T.astype(BF16)

    row = lax.broadcasted_iota(jnp.int32, (tokens, tokens), 0)
    bias_all[...] = jnp.where((row >= first) & (row <= column), 0.0, -1e30)

    def attend_one(h):
        kv = h // group
        for block in range(2):
            lo, hi = block * half, (block + 1) * half
            scores = lax.dot_general(
                kv_all[kv, :hi, :],
                q_all[h, lo:hi, :],
                (((1,), (1,)), ((), ())),
                preferred_element_type=F32,
            )
            scores = scores * HEAD ** (-0.5) + bias_all[:hi, lo:hi]
            top = jnp.max(scores, axis=0, keepdims=True)
            weights = jnp.exp(scores - top)
            total = jnp.sum(weights, axis=0, keepdims=True)
            mixed = dot(values_all[kv, :, :hi], weights.astype(BF16))
            attn_all[pl.ds(pl.multiple_of(h * HEAD, HEAD), HEAD), lo:hi] = (mixed / total).astype(BF16)

    def attend(n, carry):
        for k in range(4):
            attend_one(4 * n + k)
        return carry

    def attend_heads(lo, hi):
        for h in range(lo, hi):
            loads[2 * kv_heads + h].wait()
        lax.fori_loop(lo // 4, hi // 4, attend, 0)

    cut_one, cut_two = heads // 2, heads
    attend_heads(0, cut_one)
    for r in near_first:
        factor_gather.cross(r)
    attend_heads(cut_one, cut_two)
    z_step(2)
    attend_heads(cut_two, heads)
    for r in near_first:
        factor_gather.forward(r)

    class AllReduce:
        def __init__(self, pair_buf, x_buf, xin, yin, back):
            self.bufs = (pair_buf, x_buf, xin, yin, back)
            self.pairs = [sems.take() for _ in range(2 + (xs - 1) + (ys - 1))]
            self.kind = pair_buf.dtype

        def start(self, value):
            pair_buf = self.bufs[0]
            pair_buf[0] = value[:, :half].astype(self.kind)
            pair_buf[1] = value[:, half:].astype(self.kind)
            launch(lambda: copy(pair_buf.at[1 - c], pair_buf.at[2], self.pairs[0], partner()))

        def cross(self):
            pair_buf, x_buf, xin, yin, back = self.bufs
            arrived(pair_buf.at[2], self.pairs[0])
            x_buf[0] = (pair_buf[c].astype(F32) + pair_buf[2].astype(F32)).astype(self.kind)
            for k in range(1, xs):
                launch(lambda k=k: copy(x_buf.at[0], xin.at[k - 1], self.pairs[k], to_x(k)))

        def along(self):
            pair_buf, x_buf, xin, yin, back = self.bufs
            total = x_buf[0].astype(F32)
            for k in range(1, xs):
                arrived(xin.at[k - 1], self.pairs[k])
                total = total + xin[k - 1].astype(F32)
            x_buf[1] = total.astype(self.kind)
            for k in range(1, ys):
                launch(
                    lambda k=k: copy(x_buf.at[1], yin.at[k - 1], self.pairs[xs - 1 + k], to_y(k))
                )

        def share(self):
            pair_buf, x_buf, xin, yin, back = self.bufs
            total = x_buf[1].astype(F32)
            for k in range(1, ys):
                arrived(yin.at[k - 1], self.pairs[xs - 1 + k])
                total = total + yin[k - 1].astype(F32)
            back[c] = total.astype(self.kind)
            launch(lambda: copy(back.at[c], back.at[c], self.pairs[-1], partner()))

        def result(self):
            back = self.bufs[4]
            arrived(back.at[1 - c], self.pairs[-1])
            return jnp.concatenate([back[0], back[1]], axis=1).astype(F32)

    def expand(rank):
        return jnp.concatenate([rank * members[p] for p in range(prompts)], axis=0).astype(BF16)

    def padded(rows, full):
        return jnp.concatenate([rows, jnp.zeros((full - rows.shape[0], tokens), BF16)], axis=0)

    out_reduce = AllReduce(rank_pair, rank_x, rank_xin, rank_yin, rank_back)
    gu_reduce = AllReduce(gu_pair, gu_x, gu_xin, gu_yin, gu_back)
    attn = attn_all[...]
    out_reduce.start(dot(ao_ref[...], attn) * owned)
    for k in range(1, zs):
        arrived(wo_all.at[places[zs - k]], wo_pairs[k - 1])
    weights = jnp.concatenate([wo_all[k] for k in range(zs)], axis=1)
    base = residual_ref[...].astype(F32) + dot(weights, attn)
    middle_ref[...] = base
    gathered[c, y, x] = base.astype(BF16)
    out_reduce.cross()

    middle_gather.send()
    for n in range(ys + 4):
        if n < ys:
            middle_gather.cross(near_first[n])
        if n == 2:
            out_reduce.along()
        if n == 4:
            z_step(3)
            for r in near_first:
                factor_gather.share(r)
        if 0 <= n - 2 < ys:
            middle_gather.forward(near_first[n - 2])
        if 0 <= n - 4 < ys:
            middle_gather.share(near_first[n - 4])
        if n == ys:
            z_step(4)
            out_reduce.share()
    for r in near_first:
        factor_gather.wait(r)

    out_rank = padded(expand(ADAPTER_SCALE * out_reduce.result()), 128)
    middle_ref[...] += dot(factors[c, y, x, :, :128], out_rank)
    per_row = width // ys
    squares = jnp.zeros((8, tokens), F32)
    for r in near_first:
        middle_gather.wait(r)
        row = mod(y - r, ys)
        for core in range(CORES):
            block = factors[core, row].reshape(xs * CHUNK, 256)[:, :128]
            full = gathered[core, row].reshape(xs * CHUNK, tokens).astype(F32) + dot(block, out_rank)
            squares = squares + jnp.sum((full * full).reshape(-1, 8, tokens), axis=0)
            scaled = (full * block[:, gain_lane : gain_lane + 1].astype(F32)).astype(BF16)
            for col in range(xs):
                top = pl.multiple_of(row * per_row + (col * CORES + core) * CHUNK, CHUNK)
                normed[pl.ds(top, CHUNK), :] = scaled[col * CHUNK : (col + 1) * CHUNK]
    squares = jnp.sum(squares, axis=0, keepdims=True)
    inverse = lax.rsqrt(squares / width + EPS)

    for load in loads[2 * kv_heads + heads :]:
        load.wait()
    gu_reduce.start(dot(agu_ref[...], normed[...]) * (owned * inverse))
    for hop in range(5, ups + 1):
        z_step(hop)
    gu_reduce.cross()
    z_wait(max(ups, downs))
    weights = jnp.concatenate([gu_all[k] for k in range(zs)], axis=1)
    gu_reduce.along()
    joint_all[...] = dot(weights, normed[...]) * inverse
    hidden_factors = []
    for which in range(2):
        rows = jnp.concatenate([bgu_ref[which, slot] for slot in slots], axis=0)
        hidden_factors.append(rows.astype(F32).T.astype(BF16))
    a_rows = jnp.concatenate([ad_ref[slot] for slot in slots], axis=0)
    gu_reduce.share()
    gu_rank = gu_reduce.result()

    def hidden_correction(which, rank):
        return ADAPTER_SCALE * dot(hidden_factors[which], expand(rank))

    gate = joint_all[:hidden] + hidden_correction(0, gu_rank[:ranks])
    up = joint_all[hidden:] + hidden_correction(1, gu_rank[ranks:])
    hidden_state = (jax.nn.gelu(gate, approximate=True) * up).astype(BF16)

    shares = ADAPTER_SCALE * dot(a_rows, hidden_state)
    down_rank = jnp.concatenate(
        [shares[p * ranks : (p + 1) * ranks] * members[p] for p in range(prompts)], axis=0
    ).astype(BF16)
    source = jnp.concatenate([hidden_state, padded(down_rank, 128)], axis=0)
    share_pairs = [sems.take() for _ in range(ys)]
    near_pairs, away_pairs, on_pairs = [[sems.take() for _ in range(ys)] for _ in range(3)]
    last_pairs = [sems.take() for _ in range(ys)]
    def add_pair(r):
        arrived(pair_in.at[r], share_pairs[r])
        summed[r] = (partial[c, r].astype(F32) + pair_in[r].astype(F32)).astype(BF16)

    def begin(r):
        add_pair(r)
        way = side(r) if xs > 2 else 1
        if xs > 2:
            launch(
                lambda: copy(summed.at[r, mod(x + 2, xs)], away_in.at[r], away_pairs[r], to_x(way))
            )
        launch(
            lambda: copy(summed.at[r, mod(x - way, xs)], near_in.at[r], near_pairs[r], to_x(-way))
        )

    def carry_on(r):
        if xs > 2:
            way = side(r)
            arrived(away_in.at[r], away_pairs[r])
            total = summed[r, mod(x + way, xs)].astype(F32) + away_in[r].astype(F32)
            on_out[r] = total.astype(BF16)
            launch(lambda: copy(on_out.at[r], on_in.at[r], on_pairs[r], to_x(way)))

    def conclude(r):
        arrived(near_in.at[r], near_pairs[r])
        total = summed[r, x].astype(F32) + near_in[r].astype(F32)
        if xs > 2:
            arrived(on_in.at[r], on_pairs[r])
            total = total + on_in[r].astype(F32)
        last_out[r] = total.astype(BF16)
        if r > 0:
            launch(lambda: copy(last_out.at[r], last_in.at[r], last_pairs[r], to_y(r)))

    for n, r in enumerate(far_first):
        row = mod(y + r, ys)
        weights = down_all[pl.ds(pl.multiple_of(row * per_row, per_row), per_row), :]
        extra = jnp.concatenate(
            [factors[core, row, col, :, 128:] for col in range(xs) for core in range(CORES)], axis=0
        )
        block = dot(jnp.concatenate([weights, extra], axis=1), source).astype(BF16)
        for col in range(xs):
            for core in range(CORES):
                top = (col * CORES + core) * CHUNK
                partial[core, r, col] = block[top : top + CHUNK]
        launch(
            lambda r=r: copy(partial.at[1 - c, r], pair_in.at[r], share_pairs[r], partner())
        )
        if n >= 2:
            begin(far_first[n - 2])

    for n in range(ys - 2, ys + 4):
        if ys - 2 <= n < ys:
            begin(far_first[n])
        if n == ys - 2:
            for before in far_first[: ys - 4]:
                carry_on(before)
            for before in far_first[: ys - 6]:
                conclude(before)
        if n - 2 < ys:
            carry_on(far_first[n - 2])
        conclude(far_first[n - 4])
    total = middle_ref[...].astype(BF16).astype(F32) + last_out[0].astype(F32)
    for r in near_first[1:]:
        arrived(last_in.at[r], last_pairs[r])
        total = total + last_in[r].astype(F32)
    out_ref[...] = total.astype(BF16)
    for make in pending:
        make().wait_send()


def main_call(dims, args):
    zs, ys, xs = dims
    tokens, width = args[3].shape
    heads = width // HEAD
    kv_heads = args[4].shape[1] // (2 * HEAD)
    half = tokens // 2
    span, _, hidden = args[10].shape
    ranks = args[8].shape[0]

    def reduce_buffers(rows, kind):
        return [
            pltpu.VMEM((3, rows, half), kind),
            pltpu.VMEM((2, rows, half), kind),
            pltpu.VMEM((xs - 1, rows, half), kind),
            pltpu.VMEM((ys - 1, rows, half), kind),
            pltpu.VMEM((2, rows, half), kind),
        ]

    scratch = [
        pltpu.VMEM(args[11].shape, BF16),
        pltpu.VMEM(args[12].shape, BF16),
        pltpu.VMEM(args[14].shape, BF16),
        pltpu.VMEM((tokens, tokens), F32),
        pltpu.VMEM((2 * hidden, tokens), F32),
        pltpu.VMEM((heads, tokens, HEAD), BF16),
        pltpu.VMEM((2 * kv_heads, tokens, HEAD), BF16),
        pltpu.VMEM((kv_heads, HEAD, tokens), BF16),
        pltpu.VMEM((width, tokens), BF16),
        pltpu.VMEM((zs, CHUNK, span), BF16),
        pltpu.VMEM((zs, 2 * hidden, span), BF16),
        pltpu.VMEM((width, hidden), BF16),
        pltpu.VMEM((CORES, ys, xs, CHUNK, 256), BF16),
        pltpu.VMEM((CHUNK, tokens), F32),
        pltpu.VMEM((CORES, ys, xs, CHUNK, tokens), BF16),
        pltpu.VMEM((width, tokens), BF16),
        pltpu.VMEM((CORES, ys, xs, CHUNK, tokens), BF16),
        pltpu.VMEM((ys, xs, CHUNK, tokens), BF16),
        pltpu.VMEM((ys, xs, CHUNK, tokens), BF16),
    ]
    scratch += [pltpu.VMEM((ys, CHUNK, tokens), BF16)] * 6
    scratch += reduce_buffers(ranks, BF16)
    scratch += reduce_buffers(2 * ranks, BF16)
    scratch += [
        pltpu.SemaphoreType.DMA((heads + 2 * kv_heads + 3,)),
        pltpu.SemaphoreType.DMA((SEMAPHORES,)),
        pltpu.SemaphoreType.DMA((SEMAPHORES,)),
    ]
    smem = pl.BlockSpec(memory_space=pltpu.SMEM)
    vmem = pl.BlockSpec(memory_space=pltpu.VMEM)
    hbm = pl.BlockSpec(memory_space=pl.ANY)
    return pl.pallas_call(
        functools.partial(main_kernel, dims),
        out_shape=jax.ShapeDtypeStruct((CHUNK, tokens), BF16),
        in_specs=[smem] * 3 + [hbm] * 2 + [vmem] * 6 + [hbm] * 2 + [vmem, hbm, vmem],
        out_specs=vmem,
        scratch_shapes=scratch,
        compiler_params=pltpu.CompilerParams(
            collective_id=0, has_side_effects=True, vmem_limit_bytes=60 * 1024 * 1024
        ),
    )(*args)


def body(
    dims,
    residual_input,
    queries,
    key_value_pairs,
    prompt_length_list,
    prompt_adapter_index,
    adapter_position,
    output_matrix,
    output_factor_first,
    output_factor_second,
    norm_weight,
    gate_up_matrix,
    gate_up_factor_first,
    gate_up_factor_second,
    down_matrix,
    down_factor_first,
    down_factor_second,
):
    args = [
        prompt_length_list,
        prompt_adapter_index,
        adapter_position,
        queries,
        key_value_pairs,
        residual_input.T,
        norm_weight.reshape(1, -1),
        output_matrix.T,
        output_factor_first[0].T,
        output_factor_second.transpose(1, 2, 0),
        gate_up_matrix,
        gate_up_factor_first[0].T,
        gate_up_factor_second,
        down_matrix,
        down_factor_first.transpose(1, 2, 0),
        down_factor_second.transpose(1, 2, 0),
    ]
    return main_call(dims, args).T


def solution(mesh):
    placed = (
        P("req", "hid"),
        P("req", None),
        P("req", None),
        P("req", None),
        P("req", None),
        P(),
        P("req", "hid"),
        P("hid", None, None),
        P(None, None, "hid"),
        P("hid"),
        P("req", None, "hid"),
        P("hid", None, None),
        P(None, None, None, "hid"),
        P("hid", "req"),
        P("hid", None, None),
        P(None, None, "hid"),
    )
    dims = (mesh.shape["req"], mesh.shape["hid"] // (CORES * GRID_X), GRID_X)
    return jax.shard_map(
        functools.partial(body, dims),
        mesh=mesh,
        in_specs=placed,
        out_specs=P("req", "hid"),
        check_vma=False,
    )
```
